512 devices in a mesh: seq: 16 (over z), head: 4 (over y), req: 8 (over x, core).
Axes of the slice: x: 4, y: 4, z: 16, core: 2. Of those that a mesh axis runs over, the one named last changes fastest.
Arguments:
- pre_qkv: bfloat16 [32768, 3, 4096], P('seq', None, ('head', 'req')), may hold values from -200 to 200
- cache_kv: bfloat16 [32, 2, 1024, 4096], P('req', None, 'seq', 'head'), may hold values from -6 to 6
- dec_new: bfloat16 [128, 3, 2, 4096], P('req', None, None, 'head'), may hold values from -200 to 200
- out_weight: bfloat16 [4096, 4096], P('head', 'seq'), may hold values from -0.09375 to 0.09375
- owner_slot: int32 [32], replicated, may hold values from 0 to 127, as said below
- prompt_lengths: int32 [32], replicated, may hold values from 1 to 1024
Outputs:
- prefill_out: bfloat16 [32768, 4096], P('seq', ('head', 'req'))
- decode_out: bfloat16 [128, 2, 4096], P('req', None, ('seq', 'head'))
The draws below stay inside these ranges and needn't reach their ends.
Inputs may be any that keep to these rules, and one draw needn't show every extreme that they name: `owner_slot`: distinct slots; slot s belongs to decode group s // 16. Of the requests of one aligned block of 4, at most 2 are owned by one group, and the last group, 7, owns exactly 2 from every block.
All inputs are finite; a program needn't handle non-finite values.
Results may differ from the reference program's by a relative error of at most 0.012.
Values may be sent and summed in bfloat16 or wider, within the bound.
No kernel may reach another device: no remote copies, remote signals or barrier semaphores. Data moves between devices by JAX's collectives and lax.ppermute only.
A program may use at most 64 MiB of HBM per device.

```python
from functools import reduce
import jax
import jax.numpy as jnp
from jax import lax

D = 4096
HEADS = 32
HEAD_DIM = 128
TOK_DEV = 2048
REQ_DEV = 4
GROUPS = 8
STRETCH = 32768
FAR_STRIDE = 16
REQS = 32
SLOT_DEV = 16
SLOTS = 128
CAPACITY = 2
CACHE = 1024


def owner_table(key):
    base_key = jax.random.fold_in(key, 7)
    busy_group = GROUPS - 1
    tickets = jnp.arange(GROUPS * CAPACITY)
    ticket_group = tickets // CAPACITY

    def one_block(block_index):
        block_key = jax.random.fold_in(base_key, 100 + block_index)
        order_ints = jax.random.permutation(jax.random.fold_in(block_key, 1), GROUPS * CAPACITY)
        ticket_score = jnp.where(ticket_group == busy_group, -1, order_ints)
        chosen = jnp.argsort(ticket_score, stable=True)[:REQ_DEV]
        return jax.random.permutation(jax.random.fold_in(block_key, 2), chosen)
    picked = jax.vmap(one_block)(jnp.arange(GROUPS))

    def seat_order(group_index):
        return jax.random.permutation(jax.random.fold_in(base_key, 5000 + group_index), SLOT_DEV)
    seat_orders = jax.vmap(seat_order)(jnp.arange(GROUPS))
    dest_group = picked // CAPACITY
    seat_index = picked % CAPACITY
    blocks = jnp.arange(GROUPS)[:, None]
    place_index = seat_orders[dest_group, blocks * CAPACITY + seat_index]
    return (dest_group * SLOT_DEV + place_index).reshape(REQS).astype(jnp.int32)


def cache_field(key):
    shape = (REQS, 2, CACHE, HEADS * HEAD_DIM)
    return jnp.clip(jax.random.normal(jax.random.fold_in(key, 11), shape, jnp.float32), -6.0, 6.0)


def draw_owner_slot(key, part):
    return owner_table(key)


def draw_cache_kv(key, part):
    return cache_field(key).astype(jnp.bfloat16)


def draw_dec_new(key, part):
    width = HEADS * HEAD_DIM
    fresh_rows = jnp.clip(jax.random.normal(jax.random.fold_in(key, 13), (SLOTS, 3, 2, width), jnp.float32), -6.0, 6.0)
    return fresh_rows.astype(jnp.bfloat16)


def draw_pre_qkv(key, part):
    width = HEADS * HEAD_DIM
    field = jnp.clip(jax.random.normal(jax.random.fold_in(key, 29), (STRETCH, 3, width), jnp.float32), -6.0, 6.0)
    return field.astype(jnp.bfloat16)


def set_ends(values, key, smallest, high):
    longest = values.shape.index(max(values.shape))
    spots = []
    for shift in (0, 1):
        where = [jax.random.randint(jax.random.fold_in(key, axis), (), 0, length) for axis, length in enumerate(values.shape)]
        where[longest] = (where[longest] + shift) % values.shape[longest]
        spots.append(tuple(where))
    return values.at[spots[0]].set(smallest).at[spots[1]].set(high)


def level_of(key, dims, split, least, high):
    def one(axis_at, blocks):
        heights = jax.random.uniform(jax.random.fold_in(jax.random.fold_in(key, 6), axis_at), (blocks,), jnp.float32, least / len(split), high / len(split))
        return jnp.repeat(jnp.exp(heights), dims[axis_at] // blocks).reshape((-1,) + (1,) * (len(dims) - axis_at - 1))

    loudness = one(*split[0])
    for cut in split[1:]:
        loudness = loudness * one(*cut)
    return loudness


def scatter_about(rng, shape, scale, most, cuts=(), kind=jnp.bfloat16):
    level = level_of(rng, shape, cuts, -0.22, 0.18) if cuts else 1.0
    values = jax.random.normal(rng, shape, jnp.float32) * scale * level
    return jnp.minimum(jnp.maximum(values, -most), most).astype(kind)


def setup_inputs(seed: int = 0) -> dict:
    key_of = jax.random.split(jax.random.key(seed), 7)
    return {
        "pre_qkv": draw_pre_qkv(jax.random.fold_in(key_of[6], 71), 0),
        "cache_kv": draw_cache_kv(jax.random.fold_in(key_of[6], 71), 0),
        "dec_new": draw_dec_new(jax.random.fold_in(key_of[6], 71), 0),
        "out_weight": scatter_about(key_of[3], (HEADS * HEAD_DIM, D), (HEADS * HEAD_DIM) ** -0.5, 0.09375, ((0, 4), (1, 16))),
        "owner_slot": draw_owner_slot(jax.random.fold_in(key_of[6], 71), 0),
        "prompt_lengths": set_ends(jax.random.randint(key_of[5], (REQS,), 1, CACHE + 1), jax.random.fold_in(key_of[5], 1), 1, CACHE).astype(jnp.int32),
    }


NEG_FILL = -1e30


def partial_block(query_rows, key_rows, value_rows, allowed):
    score_scale = query_rows.shape[-1] ** -0.5
    scores = jnp.einsum("qhd,khd->hqk", query_rows.astype(jnp.float32), key_rows.astype(jnp.float32)) * score_scale
    scores = jnp.where(allowed, scores, NEG_FILL)
    peak_score = jnp.max(scores, axis=-1)
    weights = jnp.where(allowed, jnp.exp(scores - peak_score[..., None]), 0.0)
    weight_sum = jnp.sum(weights, axis=-1)
    rounded = weights.astype(jnp.bfloat16).astype(jnp.float32)
    value_sum = jnp.einsum("hqk,khd->hqd", rounded, value_rows.astype(jnp.float32))
    return peak_score, weight_sum, value_sum


def combine_levels(levels):
    top_all = reduce(jnp.maximum, [level_term[0] for level_term in levels])
    numerator = 0.0
    denominator = 0.0
    for peak_score, weight_sum, value_sum in levels:
        factor = jnp.exp(peak_score - top_all)
        denominator = denominator + weight_sum * factor
        numerator = numerator + value_sum * factor[..., None]
    return numerator / denominator[..., None]


def prefill_head(packed):
    head_query, head_key, head_value, head_number = packed
    levels = []
    for span_rows, stride in ((TOK_DEV, 1), (4 * TOK_DEV, 4), (STRETCH, FAR_STRIDE)):
        residue = (head_number % stride).astype(jnp.int32)
        segments = STRETCH // span_rows
        sparse_count = span_rows // stride

        def sparse(field):
            shaped = field.reshape(segments, sparse_count, stride, HEAD_DIM)
            return jnp.take(shaped, residue, axis=2)

        allowed = jnp.arange(sparse_count)[None, :] <= jnp.arange(sparse_count)[:, None]

        def attend(parts):
            query_part, key_part, value_part = parts
            return partial_block(query_part[:, None], key_part[:, None], value_part[:, None], allowed)

        peak_score, weight_sum, value_sum = lax.map(attend, (sparse(head_query), sparse(head_key), sparse(head_value)))
        rows_level = STRETCH // stride
        peak_rows = jnp.full((rows_level, stride), NEG_FILL, jnp.float32).at[:, residue].set(peak_score.reshape(rows_level))
        sum_rows = jnp.zeros((rows_level, stride), jnp.float32).at[:, residue].set(weight_sum.reshape(rows_level))
        value_rows = jnp.zeros((rows_level, stride, HEAD_DIM), jnp.float32).at[:, residue].set(value_sum.reshape(rows_level, HEAD_DIM))
        levels.append((peak_rows.reshape(STRETCH), sum_rows.reshape(STRETCH), value_rows.reshape(STRETCH, HEAD_DIM)))
    return combine_levels(levels)


def reference(pre_qkv, cache_kv, dec_new, out_weight, owner_slot, prompt_lengths):
    def by_head(field):
        return jnp.swapaxes(field.reshape(STRETCH, HEADS, HEAD_DIM), 0, 1)

    attended = lax.map(prefill_head, (by_head(pre_qkv[:, 0]), by_head(pre_qkv[:, 1]), by_head(pre_qkv[:, 2]), jnp.arange(HEADS, dtype=jnp.int32)))
    prefill_out = jnp.swapaxes(attended, 0, 1).reshape(STRETCH, HEADS * HEAD_DIM).astype(jnp.bfloat16)

    def decode_one(packed):
        cache_rows, fresh_rows, length = packed
        query_rows = fresh_rows[0].reshape(2, HEADS, HEAD_DIM)
        new_keys = fresh_rows[1].reshape(2, HEADS, HEAD_DIM)
        new_values = fresh_rows[2].reshape(2, HEADS, HEAD_DIM)
        cache_keys = cache_rows[0].reshape(CACHE, HEADS, HEAD_DIM)
        cache_values = cache_rows[1].reshape(CACHE, HEADS, HEAD_DIM)
        allowed = jnp.broadcast_to(jnp.arange(CACHE)[None, :] < length, (2, CACHE))
        cached_term = partial_block(query_rows, cache_keys, cache_values, allowed)
        causal = jnp.arange(2)[None, :] <= jnp.arange(2)[:, None]
        fresh_term = partial_block(query_rows, new_keys, new_values, causal)
        mixed = combine_levels([cached_term, fresh_term])
        mixed_rows = jnp.swapaxes(mixed, 0, 1).reshape(2, HEADS * HEAD_DIM).astype(jnp.bfloat16)
        return jnp.dot(mixed_rows, out_weight, preferred_element_type=jnp.float32).astype(jnp.bfloat16)

    results = lax.map(decode_one, (cache_kv, dec_new[owner_slot], prompt_lengths))
    decode_out = jnp.zeros((SLOTS, 2, D), jnp.bfloat16).at[owner_slot].set(results)
    return prefill_out, decode_out
```

```python
import functools
import math

import jax
import jax.numpy as jnp
from jax import lax
from jax.experimental import pallas as pl
from jax.experimental.pallas import tpu as pltpu
from jax.sharding import PartitionSpec as P

HD = 128
NEG = -1e30
EXP_SCALE = HD**-0.5 * math.log2(math.e)
F32 = jnp.float32
BF16 = jnp.bfloat16

VMEM = pltpu.VMEM
SMEM = pltpu.SMEM


def vspec():
    return pl.BlockSpec(memory_space=pltpu.VMEM)


def sspec():
    return pl.BlockSpec(memory_space=pltpu.SMEM)


def dot_t(a, b):
    return lax.dot_general(a, b, (((1,), (1,)), ((), ())), preferred_element_type=F32)


def dot_n(a, b):
    return lax.dot_general(a, b, (((1,), (0,)), ((), ())), preferred_element_type=F32)


def call(body, out_shape, ins, specs, scratch=(), flops=0, nbytes=0, trans=0):
    single = not isinstance(out_shape, (tuple, list))
    return pl.pallas_call(
        body,
        out_shape=out_shape,
        in_specs=specs,
        out_specs=vspec() if single else tuple(vspec() for _ in out_shape),
        scratch_shapes=list(scratch),
        compiler_params=pltpu.CompilerParams(vmem_limit_bytes=56 * 1024 * 1024),
        cost_estimate=pl.CostEstimate(flops=flops, bytes_accessed=nbytes, transcendentals=trans),
    )(*ins)


def head_id():
    return lax.axis_index("head") * lax.axis_size("req") + lax.axis_index("req")


def class_residue(c):
    j = head_id()
    r4 = lax.rem(j, 4)
    inner = lax.div(lax.rem(j, 16), 4)
    return 4 * lax.rem(c + inner, 4) + r4


def rank_in_block(own, first, k):
    grp = lax.shift_right_logical(own[first + k], 4)
    rank = jnp.int32(0)
    for e in range(k):
        rank += (lax.shift_right_logical(own[first + e], 4) == grp).astype(jnp.int32)
    return grp, rank


def route_kernel(own, dec, out, sem):
    me = lax.axis_index("req")
    copies = []
    for b in range(8):
        src = [jnp.int32(0), jnp.int32(0)]
        for k in range(4):
            slot = own[4 * b + k]
            grp, rank = rank_in_block(own, 4 * b, k)
            mine = grp == me
            for r in range(2):
                src[r] = jnp.where(mine & (rank == r), lax.rem(slot, 16), src[r])
        for r in range(2):
            cp = pltpu.make_async_copy(dec.at[src[r]], out.at[2 * b + r], sem.at[2 * b + r])
            cp.start()
            copies.append(cp)
    for cp in copies:
        cp.wait()


def pick_kernel(qkv, qm, kvm, kvf, wide):
    rows = qkv.shape[1]
    for part in range(3):
        wide[...] = qkv[part].astype(F32)
        for c in range(4):
            start = class_residue(c)
            got = wide[pl.ds(start, rows // 16, stride=16), :].astype(BF16)
            if part == 0:
                qm[pl.ds(128 * c, 128), :] = got
            else:
                kvm[pl.ds(128 * c, 128), pl.ds(128 * (part - 1), 128)] = got
                if c == 0:
                    kvf[:, pl.ds(128 * (part - 1), 128)] = got


def softmax_step(m, l, acc, s, v, mult=None):
    m_new = jnp.maximum(m, jnp.max(s, axis=1, keepdims=True))
    alpha = jnp.exp2((m - m_new) * EXP_SCALE)
    p = jnp.exp2((s - m_new) * EXP_SCALE)
    if mult is not None:
        p = p * mult
    l_new = l * alpha + jnp.sum(p, axis=1, keepdims=True)
    acc_new = acc * alpha + dot_n(p.astype(BF16), v)
    return m_new, l_new, acc_new


def near_kernel(qkv, qm, kvm, near_o, acc_o, m_o, l_o, acc_s, m_s, l_s):
    rows = qkv.shape[1]
    step = 256
    tri = lax.broadcasted_iota(jnp.int32, (step, step), 1) <= lax.broadcasted_iota(
        jnp.int32, (step, step), 0
    )
    for b in range(rows // step):
        at = pl.ds(step * b, step)
        q = qkv[0, at, :]
        s_d = jnp.where(tri, dot_t(q, qkv[1, at, :]), NEG)
        m = jnp.max(s_d, axis=1, keepdims=True)
        if b:
            s_f = dot_t(q, qkv[1, pl.ds(0, step * b), :])
            m = jnp.maximum(m, jnp.max(s_f, axis=1, keepdims=True))
        p_d = jnp.exp2((s_d - m) * EXP_SCALE)
        l = jnp.sum(p_d, axis=1, keepdims=True)
        acc = dot_n(p_d.astype(BF16), qkv[2, at, :])
        if b:
            p_f = jnp.exp2((s_f - m) * EXP_SCALE)
            l = l + jnp.sum(p_f, axis=1, keepdims=True)
            acc = acc + dot_n(p_f.astype(BF16), qkv[2, pl.ds(0, step * b), :])
        near_o[at, :] = (acc / l).astype(BF16)
        acc_s[at, :] = acc
        m_s[at, :] = jnp.broadcast_to(m, (step, HD))
        l_s[at, :] = jnp.broadcast_to(l, (step, HD))
    inner = lax.div(lax.rem(head_id(), 16), 4)

    def order(shape, dim):
        a = lax.broadcasted_iota(jnp.int32, shape, dim)
        return 4 * (a & 127) + ((lax.shift_right_logical(a, 7) + inner) & 3)

    for c in range(4):
        at = pl.ds(128 * c, 128)
        pick = pl.ds(class_residue(c), 128, stride=16)
        s = dot_t(qm[at, :], kvm[:, pl.ds(0, HD)])
        rows_at = lax.broadcasted_iota(jnp.int32, (128, 1), 0)
        row_order = 4 * rows_at + ((c + inner) & 3)
        s = jnp.where(order((1, 512), 1) <= row_order, s, NEG)
        mult = None
        if c == 0:
            mult = jnp.where(lax.broadcasted_iota(jnp.int32, (1, 512), 1) < 128, 2.0, 1.0)
        m, l, acc = softmax_step(
            m_s[pick, :][:, :1], l_s[pick, :][:, :1], acc_s[pick, :], s, kvm[:, pl.ds(HD, HD)], mult
        )
        acc_o[at, :] = acc
        m_o[at, :] = jnp.broadcast_to(m, (128, HD))
        l_o[at, :] = jnp.broadcast_to(l, (128, HD))


def far_kernel(qm, kv1, kv2, kv3, kvf, near_o, acc_i, m_i, l_i, out, acc_s, m_s, l_s, wide):
    z = lax.axis_index("seq")
    local = lax.rem(z, 4)
    group = lax.div(z, 4)
    acc_s[...] = acc_i[...]
    m_s[...] = m_i[...]
    l_s[...] = l_i[...]

    def update(rows, keys, values, mask_from=None):
        at = pl.ds(0, rows)
        s = dot_t(qm[at, :], keys)
        if mask_from is not None:
            col = lax.broadcasted_iota(jnp.int32, (1, s.shape[1]), 1)
            s = jnp.where(col < mask_from, s, NEG)
        m, l, acc = softmax_step(m_s[at, :][:, :1], l_s[at, :][:, :1], acc_s[at, :], s, values)
        acc_s[at, :] = acc
        m_s[at, :] = jnp.broadcast_to(m, (rows, HD))
        l_s[at, :] = jnp.broadcast_to(l, (rows, HD))

    for d, kv in ((1, kv1), (2, kv2), (3, kv3)):

        @pl.when(local >= d)
        def _(kv=kv):
            update(512, kv[:, pl.ds(0, HD)], kv[:, pl.ds(HD, HD)])

    for g in range(4):
        at = pl.ds(512 * g, 512)

        @pl.when(z > 4 * g)
        def _(at=at, g=g):
            update(128, kvf[at, pl.ds(0, HD)], kvf[at, pl.ds(HD, HD)], 128 * z - 512 * g)

    wide[...] = near_o[...].astype(F32)
    for c in range(4):
        at = pl.ds(128 * c, 128)
        wide[pl.ds(class_residue(c), 128, stride=16), :] = acc_s[at, :] / l_s[at, :]
    out[...] = wide[...].astype(BF16)


def pieces(x):
    hi = x.astype(BF16).astype(F32)
    rest = x - hi
    mid = rest.astype(BF16).astype(F32)
    return hi, mid, (rest - mid).astype(BF16).astype(F32)


def cache_kernel(own, lens, arr, cache, out, o_s, st_s):
    z = lax.axis_index("seq")
    me = lax.axis_index("req")
    per = cache.shape[2]
    width = cache.shape[3]
    diag = lax.shift_right_logical(
        lax.broadcasted_iota(jnp.int32, (16, width), 1), 7
    ) == lax.shift_right_logical(lax.broadcasted_iota(jnp.int32, (16, width), 0), 1)
    token = lax.broadcasted_iota(jnp.int32, (16, 16), 0) & 1
    new_col = lax.broadcasted_iota(jnp.int32, (16, 16), 1)
    new_ok = (new_col <= token) & (z == 0)
    col = z * per + lax.broadcasted_iota(jnp.int32, (16, per), 1)
    row_head = lax.shift_right_logical(lax.broadcasted_iota(jnp.int32, (16, HD), 0), 1)
    lane = lax.broadcasted_iota(jnp.int32, (16, HD), 1)
    pad = jnp.zeros((14, width), F32)
    for k in range(4):
        grp, rank = rank_in_block(own, 4 * me, k)
        row = 2 * grp + rank
        q = arr[row, 0].astype(F32)
        qd = jnp.where(diag, jnp.concatenate([q] * 8, axis=0), 0.0).astype(BF16)
        kn = jnp.concatenate([arr[row, 1].astype(F32), pad], axis=0).astype(BF16)
        vn = jnp.concatenate([arr[row, 2].astype(F32), pad], axis=0).astype(BF16)
        c_ok = col < lens[4 * me + k]
        s_c = jnp.where(c_ok, dot_t(qd, cache[k, 0]), NEG)
        s_n = jnp.where(new_ok, dot_t(qd, kn), NEG)
        m = jnp.maximum(
            jnp.max(s_c, axis=1, keepdims=True), jnp.max(s_n, axis=1, keepdims=True)
        )
        p_c = jnp.where(c_ok, jnp.exp2((s_c - m) * EXP_SCALE), 0.0)
        p_n = jnp.where(new_ok, jnp.exp2((s_n - m) * EXP_SCALE), 0.0)
        l = jnp.sum(p_c, axis=1, keepdims=True) + jnp.sum(p_n, axis=1, keepdims=True)
        full = dot_n(p_c.astype(BF16), cache[k, 1]) + dot_n(p_n.astype(BF16), vn)
        o = jnp.zeros((16, HD), F32)
        for h in range(8):
            o = jnp.where(row_head == h, full[:, HD * h : HD * (h + 1)], o)
        o = o / jnp.where(l > 0.0, l, 1.0)
        st = jnp.zeros((16, HD), F32)
        for at, piece in enumerate(pieces(m) + pieces(l)):
            st = jnp.where(lane == at, piece, st)
        for h in range(8):
            o_s[pl.ds(8 * h + 2 * k, 2), :] = o[2 * h : 2 * h + 2]
            st_s[pl.ds(8 * h + 2 * k, 2), :] = st[2 * h : 2 * h + 2]
    values = o_s[...].astype(BF16)
    turned = st_s[...].T
    stats = jnp.concatenate([turned[:16, :], jnp.zeros((16, 64), F32)], axis=1).astype(BF16)
    for t in range(out.shape[0]):
        out[t, pl.ds(0, 64), :] = values
        out[t, pl.ds(64, 16), :] = stats


def project_kernel(own, got, weight, out):
    me = lax.axis_index("req")
    count = got.shape[0]
    ms, ls = [], []
    for t in range(count):
        st = got[t, pl.ds(64, 16), :].astype(F32)
        ms.append(st[0:1] + st[1:2] + st[2:3])
        ls.append(st[3:4] + st[4:5] + st[5:6])
    m = jnp.concatenate(ms, axis=0)
    l = jnp.concatenate(ls, axis=0)
    share = jnp.exp2((m - jnp.max(m, axis=0, keepdims=True)) * EXP_SCALE) * l
    share = share / jnp.sum(share, axis=0, keepdims=True)
    share = jnp.concatenate([share, jnp.zeros((128 - count, HD), F32)], axis=0).T
    total = jnp.zeros((64, HD), F32)
    for t in range(count):
        total = total + share[:64, t : t + 1] * got[t, pl.ds(0, 64), :].astype(F32)
    rows = jnp.concatenate([total[8 * h : 8 * h + 8] for h in range(8)], axis=1)
    y = dot_n(rows.astype(BF16), weight[...])
    out[...] = jnp.zeros(out.shape, BF16)
    for k in range(4):
        grp, rank = rank_in_block(own, 4 * me, k)
        for h in range(4):
            out[16 * h + 2 * grp + rank] = y[2 * k : 2 * k + 2, 64 * h : 64 * h + 64].astype(BF16)


def settle_kernel(own, got, out):
    me = lax.axis_index("req")
    out[...] = jnp.zeros(out.shape, BF16)
    for b in range(8):
        for k in range(4):
            slot = own[4 * b + k]
            grp, rank = rank_in_block(own, 4 * b, k)

            @pl.when(grp == me)
            def _(b=b, slot=slot, rank=rank):
                total = got[2 * b + rank].astype(F32)
                for h in range(1, 4):
                    total = total + got[16 * h + 2 * b + rank].astype(F32)
                out[lax.rem(slot, 16)] = total.astype(BF16)


def shape(dims, dtype=BF16):
    return jax.ShapeDtypeStruct(dims, dtype)


def on_device(pre_qkv, cache_kv, dec_new, out_weight, owner_slot, prompt_lengths):
    qkv = jnp.swapaxes(pre_qkv, 0, 1)
    sent = pl.pallas_call(
        route_kernel,
        out_shape=shape(dec_new.shape),
        in_specs=[sspec(), pl.BlockSpec(memory_space=pl.ANY)],
        out_specs=vspec(),
        scratch_shapes=[pltpu.SemaphoreType.DMA((16,))],
        cost_estimate=pl.CostEstimate(flops=0, bytes_accessed=400000, transcendentals=0),
    )(owner_slot, dec_new)
    arrived = lax.all_to_all(sent, "req", 0, 0, tiled=True)
    qm, kvm, kvf = call(
        pick_kernel,
        (shape((512, HD)), shape((512, 2 * HD)), shape((128, 2 * HD))),
        (qkv,),
        [vspec()],
        [VMEM((2048, HD), F32)],
        nbytes=2000000,
    )
    far = lax.all_gather(kvf, "seq", axis=0, tiled=True)
    mids = [
        lax.ppermute(kvm, "seq", [(i, i + d) for i in range(16) if i % 4 + d < 4])
        for d in (1, 2, 3)
    ]
    partial = call(
        cache_kernel,
        shape((16, 80, HD)),
        (owner_slot, prompt_lengths, arrived, cache_kv),
        [sspec(), sspec(), vspec(), vspec()],
        [VMEM((64, HD), F32), VMEM((64, HD), F32)],
        flops=10**8,
        nbytes=2000000,
    )
    parts = lax.all_to_all(partial, "seq", 0, 0, tiled=True)
    state = [shape((512, HD), F32)] * 3
    near_o, acc, m, l = call(
        near_kernel,
        (shape((2048, HD)), *state),
        (qkv, qm, kvm),
        [vspec()] * 3,
        [VMEM((2048, HD), F32)] * 3,
        flops=2 * 10**9,
        nbytes=3000000,
        trans=2 * 10**6,
    )
    answers = call(
        project_kernel,
        shape((64, 2, 64)),
        (owner_slot, parts, out_weight),
        [sspec(), vspec(), vspec()],
        flops=10**7,
        nbytes=1000000,
    )
    results = lax.all_to_all(answers, ("head", "req"), 0, 0, tiled=True)
    prefill_out = call(
        far_kernel,
        shape((2048, HD)),
        (qm, *mids, far, near_o, acc, m, l),
        [vspec()] * 9,
        [VMEM((512, HD), F32)] * 3 + [VMEM((2048, HD), F32)],
        flops=10**9,
        nbytes=4000000,
        trans=10**6,
    )
    decode_out = call(
        settle_kernel,
        shape((16, 2, 64)),
        (owner_slot, results),
        [sspec(), vspec()],
        nbytes=100000,
    )
    return prefill_out, decode_out


def solution(mesh):
    return jax.shard_map(
        on_device,
        mesh=mesh,
        in_specs=(
            P("seq", None, ("head", "req")),
            P("req", None, "seq", "head"),
            P("req", None, None, "head"),
            P("head", "seq"),
            P(),
            P(),
        ),
        out_specs=(P("seq", ("head", "req")), P("req", None, ("seq", "head"))),
        check_vma=False,
    )
```

```python
import functools
import math

import jax
import jax.numpy as jnp
from jax import lax
from jax.experimental import pallas as pl
from jax.experimental.pallas import tpu as pltpu
from jax.sharding import PartitionSpec as P

HD = 128
NEG = -1e30
EXP_SCALE = HD**-0.5 * math.log2(math.e)
F32 = jnp.float32
BF16 = jnp.bfloat16

VMEM = pltpu.VMEM


def vspec():
    return pl.BlockSpec(memory_space=pltpu.VMEM)


def sspec():
    return pl.BlockSpec(memory_space=pltpu.SMEM)


def dot_t(a, b):
    return lax.dot_general(a, b, (((1,), (1,)), ((), ())), preferred_element_type=F32)


def dot_n(a, b):
    return lax.dot_general(a, b, (((1,), (0,)), ((), ())), preferred_element_type=F32)


def call(body, out_shape, ins, specs, scratch=(), vmem=24, flops=0, nbytes=0, trans=0):
    single = not isinstance(out_shape, (tuple, list))
    return pl.pallas_call(
        body,
        out_shape=out_shape,
        in_specs=specs,
        out_specs=vspec() if single else tuple(vspec() for _ in out_shape),
        scratch_shapes=list(scratch),
        compiler_params=pltpu.CompilerParams(vmem_limit_bytes=vmem * 1024 * 1024),
        cost_estimate=pl.CostEstimate(flops=flops, bytes_accessed=nbytes, transcendentals=trans),
    )(*ins)


def head_id():
    return lax.axis_index("head") * lax.axis_size("req") + lax.axis_index("req")


def class_residue(c):
    j = head_id()
    r4 = lax.rem(j, 4)
    inner = lax.div(lax.rem(j, 16), 4)
    return 4 * lax.rem(c + inner, 4) + r4


def rank_in_block(own, first, k):
    grp = lax.shift_right_logical(own[first + k], 4)
    rank = jnp.int32(0)
    for e in range(k):
        rank += (lax.shift_right_logical(own[first + e], 4) == grp).astype(jnp.int32)
    return grp, rank


def route_kernel(own, dec, out, sem):
    me = lax.axis_index("req")
    copies = []
    for b in range(8):
        src = [jnp.int32(0), jnp.int32(0)]
        for k in range(4):
            slot = own[4 * b + k]
            grp, rank = rank_in_block(own, 4 * b, k)
            mine = grp == me
            for r in range(2):
                src[r] = jnp.where(mine & (rank == r), lax.rem(slot, 16), src[r])
        for r in range(2):
            cp = pltpu.make_async_copy(dec.at[src[r]], out.at[2 * b + r], sem.at[2 * b + r])
            cp.start()
            copies.append(cp)
    for cp in copies:
        cp.wait()


def pick_kernel(qkv, qm, kvm, ask, msg, far, wide):
    rows = qkv.shape[1]
    for part in range(3):
        wide[...] = qkv[part].astype(F32)
        for c in range(4):
            start = class_residue(c)
            got = wide[pl.ds(start, rows // 16, stride=16), :].astype(BF16)
            at = pl.ds(128 * c, 128)
            if part == 0:
                qm[at, :] = got
                if c == 0:
                    ask[...] = got
                    msg[pl.ds(512, 64), pl.ds(0, HD)] = got[:64]
                    msg[pl.ds(512, 64), pl.ds(HD, HD)] = got[64:]
            else:
                lanes = pl.ds(HD * (part - 1), HD)
                kvm[at, lanes] = got
                msg[at, lanes] = got
                if c == 0:
                    far[:, lanes] = got


def softmax_step(m, l, acc, s, v, mult=None):
    m_new = jnp.maximum(m, jnp.max(s, axis=1, keepdims=True))
    alpha = jnp.exp2((m - m_new) * EXP_SCALE)
    p = jnp.exp2((s - m_new) * EXP_SCALE)
    if mult is not None:
        p = p * mult
    l_new = l * alpha + jnp.sum(p, axis=1, keepdims=True)
    acc_new = acc * alpha + dot_n(p.astype(BF16), v)
    return m_new, l_new, acc_new


def near_kernel(qkv, qm, kvm, near_o, acc_o, m_o, l_o, acc_s, m_s, l_s):
    rows = qkv.shape[1]
    step = 256
    tri = lax.broadcasted_iota(jnp.int32, (step, step), 1) <= lax.broadcasted_iota(
        jnp.int32, (step, step), 0
    )
    for b in range(rows // step):
        at = pl.ds(step * b, step)
        q = qkv[0, at, :]
        s_d = jnp.where(tri, dot_t(q, qkv[1, at, :]), NEG)
        m = jnp.max(s_d, axis=1, keepdims=True)
        if b:
            s_f = dot_t(q, qkv[1, pl.ds(0, step * b), :])
            m = jnp.maximum(m, jnp.max(s_f, axis=1, keepdims=True))
        p_d = jnp.exp2((s_d - m) * EXP_SCALE)
        l = jnp.sum(p_d, axis=1, keepdims=True)
        acc = dot_n(p_d.astype(BF16), qkv[2, at, :])
        if b:
            p_f = jnp.exp2((s_f - m) * EXP_SCALE)
            l = l + jnp.sum(p_f, axis=1, keepdims=True)
            acc = acc + dot_n(p_f.astype(BF16), qkv[2, pl.ds(0, step * b), :])
        near_o[at, :] = (acc / l).astype(BF16)
        acc_s[at, :] = acc
        m_s[at, :] = jnp.broadcast_to(m, (step, HD))
        l_s[at, :] = jnp.broadcast_to(l, (step, HD))
    inner = lax.div(lax.rem(head_id(), 16), 4)

    def order(shape, dim):
        a = lax.broadcasted_iota(jnp.int32, shape, dim)
        return 4 * (a & 127) + ((lax.shift_right_logical(a, 7) + inner) & 3)

    for c in range(4):
        at = pl.ds(128 * c, 128)
        pick = pl.ds(class_residue(c), 128, stride=16)
        s = dot_t(qm[at, :], kvm[:, pl.ds(0, HD)])
        rows_at = lax.broadcasted_iota(jnp.int32, (128, 1), 0)
        row_order = 4 * rows_at + ((c + inner) & 3)
        s = jnp.where(order((1, 512), 1) <= row_order, s, NEG)
        mult = None
        if c == 0:
            mult = jnp.where(lax.broadcasted_iota(jnp.int32, (1, 512), 1) < 128, 2.0, 1.0)
        m, l, acc = softmax_step(
            m_s[pick, :][:, :1], l_s[pick, :][:, :1], acc_s[pick, :], s, kvm[:, pl.ds(HD, HD)], mult
        )
        acc_o[at, :] = acc
        m_o[at, :] = jnp.broadcast_to(m, (128, HD))
        l_o[at, :] = jnp.broadcast_to(l, (128, HD))


def pack(rows_m, rows_l):
    count = rows_m.shape[0]
    lane = lax.broadcasted_iota(jnp.int32, (count, HD), 1)
    st = jnp.zeros((count, HD), F32)
    for at, piece in enumerate(pieces(rows_m) + pieces(rows_l)):
        st = jnp.where(lane == at, piece, st)
    blocks = [st[128 * i : 128 * i + 128].T[:8] for i in range(count // 128)]
    if len(blocks) % 2:
        blocks.append(jnp.zeros((8, HD), F32))
    return jnp.concatenate(blocks, axis=0).astype(BF16)


def unpack(rows):
    st = rows.astype(F32)
    m = st[0:1] + st[1:2] + st[2:3]
    l = st[3:4] + st[4:5] + st[5:6]
    turned = jnp.concatenate([m, l, jnp.zeros((126, HD), F32)], axis=0).T
    return turned[:, 0:1], turned[:, 1:2]


def share_kernel(
    qm, kvm, got1, got2, got3, col1, col2, col3, acc_i, m_i, l_i,
    acc_o, m_o, l_o, back1, back2, back3, acc_s, m_s, l_s,
):
    z = lax.axis_index("seq")
    local = lax.rem(z, 4)
    group = lax.div(z, 4)
    acc_s[pl.ds(0, 512), :] = acc_i[...]
    m_s[pl.ds(0, 512), :] = m_i[...]
    l_s[pl.ds(0, 512), :] = l_i[...]
    acc_s[pl.ds(512, 768), :] = jnp.zeros((768, HD), F32)
    m_s[pl.ds(512, 768), :] = jnp.full((768, HD), NEG, F32)
    l_s[pl.ds(512, 768), :] = jnp.zeros((768, HD), F32)

    def update(first, q, keys, values, twice=False):
        count = q.shape[0]
        at = pl.ds(first, count)
        s = dot_t(q, keys)
        mult = None
        if twice:
            width = s.shape[1]
            mult = jnp.where(
                (lax.broadcasted_iota(jnp.int32, (count, width), 0) < 128)
                & ((lax.broadcasted_iota(jnp.int32, (count, width), 1) & 511) < 128),
                2.0,
                1.0,
            )
        m, l, acc = softmax_step(
            m_s[at, :][:, :1], l_s[at, :][:, :1], acc_s[at, :], s, values, mult
        )
        acc_s[at, :] = acc
        m_s[at, :] = jnp.broadcast_to(m, (count, HD))
        l_s[at, :] = jnp.broadcast_to(l, (count, HD))

    own_k, own_v = kvm[:, pl.ds(0, HD)], kvm[:, pl.ds(HD, HD)]
    one = pl.ds(0, 512)
    one_k, one_v = got1[one, pl.ds(0, HD)], got1[one, pl.ds(HD, HD)]

    @pl.when((local & 1) == 1)
    def _():
        update(0, qm[...], one_k, one_v, True)

    @pl.when(local < 2)
    def _():
        update(512, got2[...], own_k, own_v, True)
        update(512, got2[...], one_k, one_v, True)

    half = pl.ds(512, 64)
    head = pl.ds(0, 128)
    queries = ((0, qm), (512, got2), (1152, got3))
    for depth, col in ((1, col1), (2, col2), (3, col3)):

        @pl.when(group >= depth)
        def _(col=col):
            k, v = col[:, pl.ds(0, HD)], col[:, pl.ds(HD, HD)]
            for first, q in queries:
                update(first, q[head, :], k, v)
            near_q = jnp.concatenate(
                [got1[half, pl.ds(0, HD)], got1[half, pl.ds(HD, HD)]], axis=0
            )
            update(1024, near_q, k, v)

    acc_o[...] = acc_s[one, :]
    m_o[...] = m_s[one, :]
    l_o[...] = l_s[one, :]
    for out, first, count in ((back2, 512, 512), (back1, 1024, 128), (back3, 1152, 128)):
        at = pl.ds(first, count)
        l = l_s[at, :]
        out[pl.ds(0, count), :] = (acc_s[at, :] / jnp.where(l > 0.0, l, 1.0)).astype(BF16)
        packed = pack(m_s[at, :], l)
        out[pl.ds(count, packed.shape[0]), :] = packed


def merge_kernel(near_o, acc, m, l, back1, back2, back3, out, wide):
    wide[...] = near_o[...].astype(F32)
    for c in range(4):
        at = pl.ds(128 * c, 128)
        terms = [(m[at, :][:, :1], l[at, :][:, :1], acc[at, :])]
        for part, rows, stat in ((back2, 128 * c, 512 + 8 * c), (back1, 0, 128), (back3, 0, 128)):
            if c and part is not back2:
                continue
            pm, plen = unpack(part[pl.ds(stat // 16 * 16, 16), :][stat % 16 : stat % 16 + 8])
            terms.append((pm, plen, part[pl.ds(rows, 128), :].astype(F32) * plen))
        top = functools.reduce(jnp.maximum, [t[0] for t in terms])
        total = 0.0
        length = 0.0
        for tm, tl, ta in terms:
            w = jnp.exp2((tm - top) * EXP_SCALE)
            length = length + tl * w
            total = total + ta * w
        wide[pl.ds(class_residue(c), 128, stride=16), :] = total / length
    out[...] = wide[...].astype(BF16)


def pieces(x):
    hi = x.astype(BF16).astype(F32)
    rest = x - hi
    mid = rest.astype(BF16).astype(F32)
    return hi, mid, (rest - mid).astype(BF16).astype(F32)


def cache_kernel(own, lens, arr, cache, out, o_s, st_s):
    z = lax.axis_index("seq")
    me = lax.axis_index("req")
    per = cache.shape[2]
    width = cache.shape[3]
    diag = lax.shift_right_logical(
        lax.broadcasted_iota(jnp.int32, (16, width), 1), 7
    ) == lax.shift_right_logical(lax.broadcasted_iota(jnp.int32, (16, width), 0), 1)
    token = lax.broadcasted_iota(jnp.int32, (16, 16), 0) & 1
    new_col = lax.broadcasted_iota(jnp.int32, (16, 16), 1)
    new_ok = (new_col <= token) & (z == 0)
    col = z * per + lax.broadcasted_iota(jnp.int32, (16, per), 1)
    row_head = lax.shift_right_logical(lax.broadcasted_iota(jnp.int32, (16, HD), 0), 1)
    lane = lax.broadcasted_iota(jnp.int32, (16, HD), 1)
    pad = jnp.zeros((14, width), F32)
    for k in range(4):
        grp, rank = rank_in_block(own, 4 * me, k)
        row = 2 * grp + rank
        q = arr[row, 0].astype(F32)
        qd = jnp.where(diag, jnp.concatenate([q] * 8, axis=0), 0.0).astype(BF16)
        kn = jnp.concatenate([arr[row, 1].astype(F32), pad], axis=0).astype(BF16)
        vn = jnp.concatenate([arr[row, 2].astype(F32), pad], axis=0).astype(BF16)
        c_ok = col < lens[4 * me + k]
        s_c = jnp.where(c_ok, dot_t(qd, cache[k, 0]), NEG)
        s_n = jnp.where(new_ok, dot_t(qd, kn), NEG)
        m = jnp.maximum(
            jnp.max(s_c, axis=1, keepdims=True), jnp.max(s_n, axis=1, keepdims=True)
        )
        p_c = jnp.where(c_ok, jnp.exp2((s_c - m) * EXP_SCALE), 0.0)
        p_n = jnp.where(new_ok, jnp.exp2((s_n - m) * EXP_SCALE), 0.0)
        l = jnp.sum(p_c, axis=1, keepdims=True) + jnp.sum(p_n, axis=1, keepdims=True)
        full = dot_n(p_c.astype(BF16), cache[k, 1]) + dot_n(p_n.astype(BF16), vn)
        o = jnp.zeros((16, HD), F32)
        for h in range(8):
            o = jnp.where(row_head == h, full[:, HD * h : HD * (h + 1)], o)
        o = o / jnp.where(l > 0.0, l, 1.0)
        st = jnp.zeros((16, HD), F32)
        for at, piece in enumerate(pieces(m) + pieces(l)):
            st = jnp.where(lane == at, piece, st)
        for h in range(8):
            o_s[pl.ds(8 * h + 2 * k, 2), :] = o[2 * h : 2 * h + 2]
            st_s[pl.ds(8 * h + 2 * k, 2), :] = st[2 * h : 2 * h + 2]
    values = o_s[...].astype(BF16)
    turned = st_s[...].T
    stats = jnp.concatenate([turned[:16, :], jnp.zeros((16, 64), F32)], axis=1).astype(BF16)
    for t in range(out.shape[0]):
        out[t, pl.ds(0, 64), :] = values
        out[t, pl.ds(64, 16), :] = stats


def project_kernel(own, got, weight, out):
    me = lax.axis_index("req")
    count = got.shape[0]
    ms, ls = [], []
    for t in range(count):
        st = got[t, pl.ds(64, 16), :].astype(F32)
        ms.append(st[0:1] + st[1:2] + st[2:3])
        ls.append(st[3:4] + st[4:5] + st[5:6])
    m = jnp.concatenate(ms, axis=0)
    l = jnp.concatenate(ls, axis=0)
    share = jnp.exp2((m - jnp.max(m, axis=0, keepdims=True)) * EXP_SCALE) * l
    share = share / jnp.sum(share, axis=0, keepdims=True)
    share = jnp.concatenate([share, jnp.zeros((128 - count, HD), F32)], axis=0).T
    total = jnp.zeros((64, HD), F32)
    for t in range(count):
        total = total + share[:64, t : t + 1] * got[t, pl.ds(0, 64), :].astype(F32)
    rows = jnp.concatenate([total[8 * h : 8 * h + 8] for h in range(8)], axis=1)
    y = dot_n(rows.astype(BF16), weight[...])
    out[...] = jnp.zeros(out.shape, BF16)
    for k in range(4):
        grp, rank = rank_in_block(own, 4 * me, k)
        for h in range(4):
            out[16 * h + 2 * grp + rank] = y[2 * k : 2 * k + 2, 64 * h : 64 * h + 64].astype(BF16)


def settle_kernel(own, got, out):
    me = lax.axis_index("req")
    out[...] = jnp.zeros(out.shape, BF16)
    for b in range(8):
        for k in range(4):
            slot = own[4 * b + k]
            grp, rank = rank_in_block(own, 4 * b, k)

            @pl.when(grp == me)
            def _(b=b, slot=slot, rank=rank):
                total = got[2 * b + rank].astype(F32)
                for h in range(1, 4):
                    total = total + got[16 * h + 2 * b + rank].astype(F32)
                out[lax.rem(slot, 16)] = total.astype(BF16)


def shape(dims, dtype=BF16):
    return jax.ShapeDtypeStruct(dims, dtype)


def staged(pre_qkv, cache_kv, dec_new, out_weight, owner_slot, prompt_lengths):
    qkv = jnp.swapaxes(pre_qkv, 0, 1)
    sent = pl.pallas_call(
        route_kernel,
        out_shape=shape(dec_new.shape),
        in_specs=[sspec(), pl.BlockSpec(memory_space=pl.ANY)],
        out_specs=vspec(),
        scratch_shapes=[pltpu.SemaphoreType.DMA((16,))],
        cost_estimate=pl.CostEstimate(flops=0, bytes_accessed=400000, transcendentals=0),
    )(owner_slot, dec_new)
    arrived = lax.all_to_all(sent, "req", 0, 0, tiled=True)
    qm, kvm, ask, msg, far = call(
        pick_kernel,
        (
            shape((512, HD)),
            shape((512, 2 * HD)),
            shape((128, HD)),
            shape((576, 2 * HD)),
            shape((128, 2 * HD)),
        ),
        (qkv,),
        [vspec()],
        [VMEM((2048, HD), F32)],
        nbytes=4000000,
    )

    def swap(x, bits):
        return lax.ppermute(x, "seq", [(i, i ^ bits) for i in range(16)])

    def relay(x, first):
        return lax.ppermute(x, "seq", [(i, i + 4) for i in range(first, 12)])

    col1 = relay(far, 0)
    got1 = swap(msg, 1)
    got2 = swap(qm, 2)
    got3 = swap(ask, 3)
    partial = call(
        cache_kernel,
        shape((16, 80, HD)),
        (owner_slot, prompt_lengths, arrived, cache_kv),
        [sspec(), sspec(), vspec(), vspec()],
        [VMEM((64, HD), F32), VMEM((64, HD), F32)],
        flops=10**8,
        nbytes=2000000,
    )
    parts = lax.all_to_all(partial, "seq", 0, 0, tiled=True)
    col2 = relay(col1, 4)
    state = [shape((512, HD), F32)] * 3
    near_o, acc, m, l = call(
        near_kernel,
        (shape((2048, HD)), *state),
        (qkv, qm, kvm),
        [vspec()] * 3,
        [VMEM((2048, HD), F32)] * 3,
        flops=2 * 10**9,
        nbytes=3000000,
        trans=2 * 10**6,
    )
    col3 = relay(col2, 8)
    acc, m, l, back1, back2, back3 = call(
        share_kernel,
        (*state, shape((144, HD)), shape((544, HD)), shape((144, HD))),
        (qm, kvm, got1, got2, got3, col1, col2, col3, acc, m, l),
        [vspec()] * 11,
        [VMEM((1280, HD), F32)] * 3,
        flops=10**9,
        nbytes=4000000,
        trans=10**6,
    )
    back1 = swap(back1, 1)
    back2 = swap(back2, 2)
    back3 = swap(back3, 3)
    answers = call(
        project_kernel,
        shape((64, 2, 64)),
        (owner_slot, parts, out_weight),
        [sspec(), vspec(), vspec()],
        flops=10**7,
        nbytes=1000000,
    )
    results = lax.all_to_all(answers, ("head", "req"), 0, 0, tiled=True)
    prefill_out = call(
        merge_kernel,
        shape((2048, HD)),
        (near_o, acc, m, l, back1, back2, back3),
        [vspec()] * 7,
        [VMEM((2048, HD), F32)],
        flops=10**8,
        nbytes=4000000,
    )
    decode_out = call(
        settle_kernel,
        shape((16, 2, 64)),
        (owner_slot, results),
        [sspec(), vspec()],
        nbytes=100000,
    )
    return prefill_out, decode_out


def solution(mesh):
    return jax.shard_map(
        staged,
        mesh=mesh,
        in_specs=(
            P("seq", None, ("head", "req")),
            P("req", None, "seq", "head"),
            P("req", None, None, "head"),
            P("head", "seq"),
            P(),
            P(),
        ),
        out_specs=(P("seq", ("head", "req")), P("req", None, ("seq", "head"))),
        check_vma=False,
    )
```

```python
import functools
import math

import jax
import jax.numpy as jnp
from jax import lax
from jax.experimental import pallas as pl
from jax.experimental.pallas import tpu as pltpu
from jax.sharding import PartitionSpec as P

HD = 128
NEG = -1e30
EXP_SCALE = HD**-0.5 * math.log2(math.e)
F32 = jnp.float32
BF16 = jnp.bfloat16

VMEM = pltpu.VMEM


def vspec():
    return pl.BlockSpec(memory_space=pltpu.VMEM)


def far_memory(x):
    return pltpu.with_memory_space_constraint(x, pltpu.HBM)


def hspec():
    return pl.BlockSpec(memory_space=pltpu.HBM)


def sspec():
    return pl.BlockSpec(memory_space=pltpu.SMEM)


def dot_t(a, b):
    return lax.dot_general(a, b, (((1,), (1,)), ((), ())), preferred_element_type=F32)


def dot_n(a, b):
    return lax.dot_general(a, b, (((1,), (0,)), ((), ())), preferred_element_type=F32)


def call(body, out_shape, ins, specs, scratch=(), vmem=24, flops=0, nbytes=0, trans=0, outs=None):
    single = not isinstance(out_shape, (tuple, list))
    return pl.pallas_call(
        body,
        out_shape=out_shape,
        in_specs=specs,
        out_specs=vspec() if single else tuple(outs or [vspec() for _ in out_shape]),
        scratch_shapes=list(scratch),
        compiler_params=pltpu.CompilerParams(vmem_limit_bytes=vmem * 1024 * 1024),
        cost_estimate=pl.CostEstimate(flops=flops, bytes_accessed=nbytes, transcendentals=trans),
    )(*ins)


def head_id():
    return lax.axis_index("head") * lax.axis_size("req") + lax.axis_index("req")


def class_residue(c):
    j = head_id()
    r4 = lax.rem(j, 4)
    inner = lax.div(lax.rem(j, 16), 4)
    return 4 * lax.rem(c + inner, 4) + r4


def rank_in_block(own, first, k):
    grp = lax.shift_right_logical(own[first + k], 4)
    rank = jnp.int32(0)
    for e in range(k):
        rank += (lax.shift_right_logical(own[first + e], 4) == grp).astype(jnp.int32)
    return grp, rank


def start_kernel(own, dec, qkv, sent, qm, kvm, ask, msg, far, raw, wide, sem, part_sem):
    me = lax.axis_index("req")
    rows = qkv.shape[1]
    parts = []
    for part in range(3):
        cp = pltpu.make_async_copy(qkv.at[part], raw.at[part], part_sem.at[part])
        cp.start()
        parts.append(cp)
    copies = []
    for b in range(8):
        src = [jnp.int32(0), jnp.int32(0)]
        for k in range(4):
            slot = own[4 * b + k]
            grp, rank = rank_in_block(own, 4 * b, k)
            mine = grp == me
            for r in range(2):
                src[r] = jnp.where(mine & (rank == r), slot & 15, src[r])
        for r in range(2):
            cp = pltpu.make_async_copy(dec.at[src[r]], sent.at[2 * b + r], sem.at[2 * b + r])
            cp.start()
            copies.append(cp)
    for part in range(3):
        parts[part].wait()
        wide[...] = raw[part].astype(F32)
        for c in range(4):
            start = class_residue(c)
            got = wide[pl.ds(start, rows // 16, stride=16), :].astype(BF16)
            at = pl.ds(128 * c, 128)
            if part == 0:
                qm[at, :] = got
                if c == 0:
                    ask[...] = got
                    msg[pl.ds(512, 64), pl.ds(0, HD)] = got[:64]
                    msg[pl.ds(512, 64), pl.ds(HD, HD)] = got[64:]
            else:
                lanes = pl.ds(HD * (part - 1), HD)
                kvm[at, lanes] = got
                msg[at, lanes] = got
                if c == 0:
                    far[:, lanes] = got
    for cp in copies:
        cp.wait()


def softmax_step(m, l, acc, s, v, mult=None):
    m_new = jnp.maximum(m, jnp.max(s, axis=1, keepdims=True))
    alpha = jnp.exp2((m - m_new) * EXP_SCALE)
    p = jnp.exp2((s - m_new) * EXP_SCALE)
    if mult is not None:
        p = p * mult
    l_new = l * alpha + jnp.sum(p, axis=1, keepdims=True)
    acc_new = acc * alpha + dot_n(p.astype(BF16), v)
    return m_new, l_new, acc_new


def both(m, l):
    count = m.shape[0]
    lane = lax.broadcasted_iota(jnp.int32, (count, HD), 1)
    return jnp.where(lane == 0, m, l)


def near_kernel(
    qkv, qm, kvm, near_h, acc_h, ml_h, raw, acc_s, ml_s, near_o, acc_o, ml_o, sem, out_sem
):
    rows = qkv.shape[1]
    step = 256
    copies = []
    for b in range(rows // step):
        at = pl.ds(step * b, step)
        cp = pltpu.make_async_copy(qkv.at[:, at, :], raw.at[:, at, :], sem.at[b])
        cp.start()
        copies.append(cp)
    tri = lax.broadcasted_iota(jnp.int32, (step, step), 1) <= lax.broadcasted_iota(
        jnp.int32, (step, step), 0
    )
    for b in range(rows // step):
        at = pl.ds(step * b, step)
        copies[b].wait()
        q = raw[0, at, :]
        s_d = jnp.where(tri, dot_t(q, raw[1, at, :]), NEG)
        m = jnp.max(s_d, axis=1, keepdims=True)
        if b:
            s_f = dot_t(q, raw[1, pl.ds(0, step * b), :])
            m = jnp.maximum(m, jnp.max(s_f, axis=1, keepdims=True))
        p_d = jnp.exp2((s_d - m) * EXP_SCALE)
        l = jnp.sum(p_d, axis=1, keepdims=True)
        acc = dot_n(p_d.astype(BF16), raw[2, at, :])
        if b:
            p_f = jnp.exp2((s_f - m) * EXP_SCALE)
            l = l + jnp.sum(p_f, axis=1, keepdims=True)
            acc = acc + dot_n(p_f.astype(BF16), raw[2, pl.ds(0, step * b), :])
        near_o[at, :] = (acc / l).astype(BF16)
        cp = pltpu.make_async_copy(near_o.at[at], near_h.at[at], out_sem.at[b])
        cp.start()
        copies.append(cp)
        acc_s[at, :] = acc
        ml_s[at, :] = both(m, l)
    inner = lax.div(lax.rem(head_id(), 16), 4)

    def order(shape, dim):
        a = lax.broadcasted_iota(jnp.int32, shape, dim)
        return 4 * (a & 127) + ((lax.shift_right_logical(a, 7) + inner) & 3)

    for c in range(4):
        at = pl.ds(128 * c, 128)
        pick = pl.ds(class_residue(c), 128, stride=16)
        s = dot_t(qm[at, :], kvm[:, pl.ds(0, HD)])
        rows_at = lax.broadcasted_iota(jnp.int32, (128, 1), 0)
        row_order = 4 * rows_at + ((c + inner) & 3)
        s = jnp.where(order((1, 512), 1) <= row_order, s, NEG)
        mult = None
        if c == 0:
            mult = jnp.where(lax.broadcasted_iota(jnp.int32, (1, 512), 1) < 128, 2.0, 1.0)
        ml = ml_s[pick, :]
        m, l, acc = softmax_step(
            ml[:, 0:1], ml[:, 1:2], acc_s[pick, :], s, kvm[:, pl.ds(HD, HD)], mult
        )
        acc_o[at, :] = acc
        ml_o[at, :] = both(m, l)
    for i, (src, dst) in enumerate(((acc_o, acc_h), (ml_o, ml_h))):
        cp = pltpu.make_async_copy(src, dst, sem.at[i])
        cp.start()
        copies.append(cp)
    for cp in copies[rows // step :]:
        cp.wait()


def pack(rows_m, rows_l):
    count = rows_m.shape[0]
    lane = lax.broadcasted_iota(jnp.int32, (count, HD), 1)
    st = jnp.zeros((count, HD), F32)
    for at, piece in enumerate(pieces(rows_m) + pieces(rows_l)):
        st = jnp.where(lane == at, piece, st)
    blocks = [st[128 * i : 128 * i + 128].T[:8] for i in range(count // 128)]
    if len(blocks) % 2:
        blocks.append(jnp.zeros((8, HD), F32))
    return jnp.concatenate(blocks, axis=0).astype(BF16)


def unpack(rows):
    st = rows.astype(F32)
    m = st[0:1] + st[1:2] + st[2:3]
    l = st[3:4] + st[4:5] + st[5:6]
    turned = jnp.concatenate([m, l, jnp.zeros((126, HD), F32)], axis=0).T
    return turned[:, 0:1], turned[:, 1:2]


def share_kernel(
    qm, kvm, got1, got2, got3, col1, col2, col3, acc_i, ml_i,
    acc_o, ml_o, back1, back2, back3, acc_s, ml_s, sem,
):
    z = lax.axis_index("seq")
    local = lax.rem(z, 4)
    group = lax.div(z, 4)
    one = pl.ds(0, 512)
    load_acc = pltpu.make_async_copy(acc_i, acc_s.at[one], sem.at[0])
    load_ml = pltpu.make_async_copy(ml_i, ml_s.at[one], sem.at[1])
    load_acc.start()
    load_ml.start()
    rest = pl.ds(512, 768)
    acc_s[rest, :] = jnp.zeros((768, HD), F32)
    ml_s[rest, :] = both(jnp.full((768, 1), NEG, F32), jnp.zeros((768, 1), F32))

    def update(first, q, keys, values, twice=False):
        count = q.shape[0]
        at = pl.ds(first, count)
        s = dot_t(q, keys)
        mult = None
        if twice:
            width = s.shape[1]
            mult = jnp.where(
                (lax.broadcasted_iota(jnp.int32, (count, width), 0) < 128)
                & ((lax.broadcasted_iota(jnp.int32, (count, width), 1) & 511) < 128),
                2.0,
                1.0,
            )
        ml = ml_s[at, :]
        m, l, acc = softmax_step(ml[:, 0:1], ml[:, 1:2], acc_s[at, :], s, values, mult)
        acc_s[at, :] = acc
        ml_s[at, :] = both(m, l)

    own_k, own_v = kvm[:, pl.ds(0, HD)], kvm[:, pl.ds(HD, HD)]
    one_k, one_v = got1[one, pl.ds(0, HD)], got1[one, pl.ds(HD, HD)]

    @pl.when(local < 2)
    def _():
        update(512, got2[...], own_k, own_v, True)
        update(512, got2[...], one_k, one_v, True)

    load_acc.wait()
    load_ml.wait()

    @pl.when((local & 1) == 1)
    def _():
        update(0, qm[...], one_k, one_v, True)

    half = pl.ds(512, 64)
    head = pl.ds(0, 128)
    queries = ((0, qm), (512, got2), (1152, got3))
    for depth, col in ((1, col1), (2, col2), (3, col3)):

        @pl.when(group >= depth)
        def _(col=col):
            k, v = col[:, pl.ds(0, HD)], col[:, pl.ds(HD, HD)]
            for first, q in queries:
                update(first, q[head, :], k, v)
            near_q = jnp.concatenate(
                [got1[half, pl.ds(0, HD)], got1[half, pl.ds(HD, HD)]], axis=0
            )
            update(1024, near_q, k, v)

    save_acc = pltpu.make_async_copy(acc_s.at[one], acc_o, sem.at[0])
    save_ml = pltpu.make_async_copy(ml_s.at[one], ml_o, sem.at[1])
    save_acc.start()
    save_ml.start()
    for out, first, count in ((back2, 512, 512), (back1, 1024, 128), (back3, 1152, 128)):
        at = pl.ds(first, count)
        ml = ml_s[at, :]
        m, l = ml[:, 0:1], ml[:, 1:2]
        out[pl.ds(0, count), :] = (acc_s[at, :] / jnp.where(l > 0.0, l, 1.0)).astype(BF16)
        packed = pack(m, l)
        out[pl.ds(count, packed.shape[0]), :] = packed
    save_acc.wait()
    save_ml.wait()


def merge_kernel(near_h, acc_h, ml_h, back1, back2, back3, out, near, acc, ml, wide, sem):
    copies = [
        pltpu.make_async_copy(src, dst, sem.at[i])
        for i, (src, dst) in enumerate(((near_h, near), (acc_h, acc), (ml_h, ml)))
    ]
    for cp in copies:
        cp.start()
    for cp in copies:
        cp.wait()
    wide[...] = near[...].astype(F32)
    for c in range(4):
        at = pl.ds(128 * c, 128)
        terms = [(ml[at, :][:, 0:1], ml[at, :][:, 1:2], acc[at, :])]
        for part, rows, stat in ((back2, 128 * c, 512 + 8 * c), (back1, 0, 128), (back3, 0, 128)):
            if c and part is not back2:
                continue
            pm, plen = unpack(part[pl.ds(stat // 16 * 16, 16), :][stat % 16 : stat % 16 + 8])
            terms.append((pm, plen, part[pl.ds(rows, 128), :].astype(F32) * plen))
        top = functools.reduce(jnp.maximum, [t[0] for t in terms])
        total = 0.0
        length = 0.0
        for tm, tl, ta in terms:
            w = jnp.exp2((tm - top) * EXP_SCALE)
            length = length + tl * w
            total = total + ta * w
        wide[pl.ds(class_residue(c), 128, stride=16), :] = total / length
    out[...] = wide[...].astype(BF16)


def pieces(x):
    hi = x.astype(BF16).astype(F32)
    rest = x - hi
    mid = rest.astype(BF16).astype(F32)
    return hi, mid, (rest - mid).astype(BF16).astype(F32)


def cache_kernel(own, lens, arr, cache_h, out, cache, o_s, st_s, sem):
    copies = []
    for k in range(4):
        cp = pltpu.make_async_copy(cache_h.at[k], cache.at[k], sem.at[k])
        cp.start()
        copies.append(cp)
    z = lax.axis_index("seq")
    me = lax.axis_index("req")
    per = cache.shape[2]
    width = cache.shape[3]
    diag = lax.shift_right_logical(
        lax.broadcasted_iota(jnp.int32, (16, width), 1), 7
    ) == lax.shift_right_logical(lax.broadcasted_iota(jnp.int32, (16, width), 0), 1)
    token = lax.broadcasted_iota(jnp.int32, (16, 16), 0) & 1
    new_col = lax.broadcasted_iota(jnp.int32, (16, 16), 1)
    new_ok = (new_col <= token) & (z == 0)
    col = z * per + lax.broadcasted_iota(jnp.int32, (16, per), 1)
    row_head = lax.shift_right_logical(lax.broadcasted_iota(jnp.int32, (16, HD), 0), 1)
    lane = lax.broadcasted_iota(jnp.int32, (16, HD), 1)
    pad = jnp.zeros((14, width), F32)
    for k in range(4):
        grp, rank = rank_in_block(own, 4 * me, k)
        row = 2 * grp + rank
        q = arr[row, 0].astype(F32)
        qd = jnp.where(diag, jnp.concatenate([q] * 8, axis=0), 0.0).astype(BF16)
        kn = jnp.concatenate([arr[row, 1].astype(F32), pad], axis=0).astype(BF16)
        vn = jnp.concatenate([arr[row, 2].astype(F32), pad], axis=0).astype(BF16)
        c_ok = col < lens[4 * me + k]
        copies[k].wait()
        s_c = jnp.where(c_ok, dot_t(qd, cache[k, 0]), NEG)
        s_n = jnp.where(new_ok, dot_t(qd, kn), NEG)
        m = jnp.maximum(
            jnp.max(s_c, axis=1, keepdims=True), jnp.max(s_n, axis=1, keepdims=True)
        )
        p_c = jnp.where(c_ok, jnp.exp2((s_c - m) * EXP_SCALE), 0.0)
        p_n = jnp.where(new_ok, jnp.exp2((s_n - m) * EXP_SCALE), 0.0)
        l = jnp.sum(p_c, axis=1, keepdims=True) + jnp.sum(p_n, axis=1, keepdims=True)
        full = dot_n(p_c.astype(BF16), cache[k, 1]) + dot_n(p_n.astype(BF16), vn)
        o = jnp.zeros((16, HD), F32)
        for h in range(8):
            o = jnp.where(row_head == h, full[:, HD * h : HD * (h + 1)], o)
        o = o / jnp.where(l > 0.0, l, 1.0)
        st = jnp.zeros((16, HD), F32)
        for at, piece in enumerate(pieces(m) + pieces(l)):
            st = jnp.where(lane == at, piece, st)
        for h in range(8):
            o_s[pl.ds(8 * h + 2 * k, 2), :] = o[2 * h : 2 * h + 2]
            st_s[pl.ds(8 * h + 2 * k, 2), :] = st[2 * h : 2 * h + 2]
    values = o_s[...].astype(BF16)
    turned = st_s[...].T
    stats = jnp.concatenate([turned[:16, :], jnp.zeros((16, 64), F32)], axis=1).astype(BF16)
    for t in range(out.shape[0]):
        out[t, pl.ds(0, 64), :] = values
        out[t, pl.ds(64, 16), :] = stats


def project_kernel(own, got, weight, out):
    me = lax.axis_index("req")
    count = got.shape[0]
    ms, ls = [], []
    for t in range(count):
        st = got[t, pl.ds(64, 16), :].astype(F32)
        ms.append(st[0:1] + st[1:2] + st[2:3])
        ls.append(st[3:4] + st[4:5] + st[5:6])
    m = jnp.concatenate(ms, axis=0)
    l = jnp.concatenate(ls, axis=0)
    share = jnp.exp2((m - jnp.max(m, axis=0, keepdims=True)) * EXP_SCALE) * l
    share = share / jnp.sum(share, axis=0, keepdims=True)
    share = jnp.concatenate([share, jnp.zeros((128 - count, HD), F32)], axis=0).T
    total = jnp.zeros((64, HD), F32)
    for t in range(count):
        total = total + share[:64, t : t + 1] * got[t, pl.ds(0, 64), :].astype(F32)
    rows = jnp.concatenate([total[8 * h : 8 * h + 8] for h in range(8)], axis=1)
    y = dot_n(rows.astype(BF16), weight[...])
    out[...] = jnp.zeros(out.shape, BF16)
    seats = [rank_in_block(own, 4 * me, k) for k in range(4)]
    for h in range(4):
        cols = slice(64 * h, 64 * h + 64)
        lines = [
            jnp.concatenate([y[2 * k : 2 * k + 1, cols], y[2 * k + 1 : 2 * k + 2, cols]], axis=1)
            for k in range(4)
        ]
        for grp, _ in seats:
            pair = [jnp.zeros((1, HD), F32)] * 2
            for (other, rank), line in zip(seats, lines):
                for r in range(2):
                    pair[r] = jnp.where((other == grp) & (rank == r), line, pair[r])
            out[8 * h + grp] = jnp.concatenate(pair, axis=0).astype(BF16)


def settle_kernel(own, got, out):
    me = lax.axis_index("req")
    total = got[pl.ds(0, 8)].astype(F32)
    for h in range(1, 4):
        total = total + got[pl.ds(8 * h, 8)].astype(F32)
    out[...] = jnp.zeros(out.shape, BF16)
    for b in range(8):
        first = total[b]
        for k in range(4):
            slot = own[4 * b + k]
            grp, rank = rank_in_block(own, 4 * b, k)

            @pl.when(grp == me)
            def _(first=first, slot=slot, rank=rank):
                row = jnp.where(rank == 0, first[0:1], first[1:2])
                out[slot & 15] = jnp.concatenate([row[:, :64], row[:, 64:]], axis=0).astype(BF16)


def shape(dims, dtype=BF16):
    return jax.ShapeDtypeStruct(dims, dtype)


def staged(pre_qkv, cache_kv, dec_new, out_weight, owner_slot, prompt_lengths):
    qkv = jnp.swapaxes(pre_qkv, 0, 1)
    sent, qm, kvm, ask, msg, far = call(
        start_kernel,
        (
            shape(dec_new.shape),
            shape((512, HD)),
            shape((512, 2 * HD)),
            shape((128, HD)),
            shape((576, 2 * HD)),
            shape((128, 2 * HD)),
        ),
        (owner_slot, far_memory(dec_new), far_memory(qkv)),
        [sspec(), hspec(), hspec()],
        [
            VMEM((3, 2048, HD), BF16),
            VMEM((2048, HD), F32),
            pltpu.SemaphoreType.DMA((16,)),
            pltpu.SemaphoreType.DMA((3,)),
        ],
        nbytes=4000000,
    )
    arrived = lax.all_to_all(sent, "req", 0, 0, tiled=True)

    def swap(x, bits):
        return lax.ppermute(x, "seq", [(i, i ^ bits) for i in range(16)])

    def relay(x, first):
        return lax.ppermute(x, "seq", [(i, i + 4) for i in range(first, 12)])

    col1 = relay(far, 0)
    got3 = swap(ask, 3)
    got2 = swap(qm, 2)
    got1 = swap(msg, 1)
    partial = call(
        cache_kernel,
        shape((16, 80, HD)),
        (owner_slot, prompt_lengths, arrived, far_memory(cache_kv)),
        [sspec(), sspec(), vspec(), hspec()],
        [
            VMEM(cache_kv.shape, BF16),
            VMEM((64, HD), F32),
            VMEM((64, HD), F32),
            pltpu.SemaphoreType.DMA((4,)),
        ],
        flops=10**8,
        nbytes=2000000,
    )
    parts = lax.all_to_all(partial, "seq", 0, 0, tiled=True)
    col2 = relay(col1, 4)
    state = [pltpu.HBM((512, HD), F32)] * 2
    near_o, acc, ml = call(
        near_kernel,
        (pltpu.HBM((2048, HD), BF16), *state),
        (far_memory(qkv), qm, kvm),
        [hspec(), vspec(), vspec()],
        [
            VMEM((3, 2048, HD), BF16),
            VMEM((2048, HD), F32),
            VMEM((2048, HD), F32),
            VMEM((2048, HD), BF16),
            VMEM((512, HD), F32),
            VMEM((512, HD), F32),
            pltpu.SemaphoreType.DMA((8,)),
            pltpu.SemaphoreType.DMA((8,)),
        ],
        flops=2 * 10**9,
        nbytes=3000000,
        trans=2 * 10**6,
        outs=[hspec(), hspec(), hspec()],
    )
    col3 = relay(col2, 8)
    acc, ml, back1, back2, back3 = call(
        share_kernel,
        (*state, shape((144, HD)), shape((544, HD)), shape((144, HD))),
        (qm, kvm, got1, got2, got3, col1, col2, col3, far_memory(acc), far_memory(ml)),
        [vspec()] * 8 + [hspec()] * 2,
        [VMEM((1280, HD), F32)] * 2 + [pltpu.SemaphoreType.DMA((2,))],
        flops=10**9,
        nbytes=4000000,
        trans=10**6,
        outs=[hspec()] * 2 + [vspec()] * 3,
    )
    back1 = swap(back1, 1)
    back3 = swap(back3, 3)
    back2 = swap(back2, 2)
    answers = call(
        project_kernel,
        shape((32, 2, HD)),
        (owner_slot, parts, out_weight),
        [sspec(), vspec(), vspec()],
        flops=10**7,
        nbytes=1000000,
    )
    results = lax.all_to_all(answers, ("head", "req"), 0, 0, tiled=True)
    prefill_out = call(
        merge_kernel,
        shape((2048, HD)),
        (far_memory(near_o), far_memory(acc), far_memory(ml), back1, back2, back3),
        [hspec()] * 3 + [vspec()] * 3,
        [
            VMEM((2048, HD), BF16),
            VMEM((512, HD), F32),
            VMEM((512, HD), F32),
            VMEM((2048, HD), F32),
            pltpu.SemaphoreType.DMA((3,)),
        ],
        flops=10**8,
        nbytes=4000000,
    )
    decode_out = call(
        settle_kernel,
        shape((16, 2, 64)),
        (owner_slot, results),
        [sspec(), vspec()],
        nbytes=100000,
    )
    return prefill_out, decode_out


def solution(mesh):
    return jax.shard_map(
        staged,
        mesh=mesh,
        in_specs=(
            P("seq", None, ("head", "req")),
            P("req", None, "seq", "head"),
            P("req", None, None, "head"),
            P("head", "seq"),
            P(),
            P(),
        ),
        out_specs=(P("seq", ("head", "req")), P("req", None, ("seq", "head"))),
        check_vma=False,
    )
```

```python
import functools
import math

import jax
import jax.numpy as jnp
from jax import lax
from jax.experimental import pallas as pl
from jax.experimental.pallas import tpu as pltpu
from jax.sharding import PartitionSpec as P

HD = 128
NEG = -1e30
EXP_SCALE = HD**-0.5 * math.log2(math.e)
F32 = jnp.float32
BF16 = jnp.bfloat16

VMEM = pltpu.VMEM
SMEM = pltpu.SMEM


def vspec():
    return pl.BlockSpec(memory_space=pltpu.VMEM)


def far_memory(x):
    return pltpu.with_memory_space_constraint(x, pltpu.HBM)


def hspec():
    return pl.BlockSpec(memory_space=pltpu.HBM)


def sspec():
    return pl.BlockSpec(memory_space=pltpu.SMEM)


def dot_t(a, b):
    return lax.dot_general(a, b, (((1,), (1,)), ((), ())), preferred_element_type=F32)


def dot_n(a, b):
    return lax.dot_general(a, b, (((1,), (0,)), ((), ())), preferred_element_type=F32)


def call(body, out_shape, ins, specs, scratch=(), vmem=24, flops=0, nbytes=0, trans=0, outs=None):
    single = not isinstance(out_shape, (tuple, list))
    return pl.pallas_call(
        body,
        out_shape=out_shape,
        in_specs=specs,
        out_specs=vspec() if single else tuple(outs or [vspec() for _ in out_shape]),
        scratch_shapes=list(scratch),
        compiler_params=pltpu.CompilerParams(vmem_limit_bytes=vmem * 1024 * 1024),
        cost_estimate=pl.CostEstimate(flops=flops, bytes_accessed=nbytes, transcendentals=trans),
    )(*ins)


def head_id():
    return lax.axis_index("head") * lax.axis_size("req") + lax.axis_index("req")


def class_residue(c):
    j = head_id()
    r4 = lax.rem(j, 4)
    inner = lax.div(lax.rem(j, 16), 4)
    return 4 * lax.rem(c + inner, 4) + r4


def rank_in_block(own, first, k):
    grp = lax.shift_right_logical(own[first + k], 4)
    rank = jnp.int32(0)
    for e in range(k):
        rank += (lax.shift_right_logical(own[first + e], 4) == grp).astype(jnp.int32)
    return grp, rank


def start_kernel(
    own_h, dec, qkv, raw, sent, qm, ask, msg, far, own, wide, sem, part_sem, own_sem
):
    own_copy = pltpu.make_async_copy(own_h, own, own_sem)
    own_copy.start()
    me = lax.axis_index("req")
    rows = qkv.shape[1]
    parts = []
    for part in range(3):
        cp = pltpu.make_async_copy(qkv.at[part], raw.at[part], part_sem.at[part])
        cp.start()
        parts.append(cp)
    copies = []
    own_copy.wait()
    for b in range(8):
        src = [jnp.int32(0), jnp.int32(0)]
        for k in range(4):
            slot = own[4 * b + k]
            grp, rank = rank_in_block(own, 4 * b, k)
            mine = grp == me
            for r in range(2):
                src[r] = jnp.where(mine & (rank == r), slot & 15, src[r])
        for r in range(2):
            cp = pltpu.make_async_copy(dec.at[src[r]], sent.at[2 * b + r], sem.at[2 * b + r])
            cp.start()
            copies.append(cp)
    for part in range(3):
        parts[part].wait()
        wide[...] = raw[part].astype(F32)
        for c in range(4):
            start = class_residue(c)
            got = wide[pl.ds(start, rows // 16, stride=16), :].astype(BF16)
            at = pl.ds(128 * c, 128)
            if part == 0:
                qm[at, :] = got
                if c == 0:
                    ask[...] = got
                    msg[pl.ds(512, 64), pl.ds(0, HD)] = got[:64]
                    msg[pl.ds(512, 64), pl.ds(HD, HD)] = got[64:]
            else:
                lanes = pl.ds(HD * (part - 1), HD)
                msg[at, lanes] = got
                if c == 0:
                    far[:, lanes] = got
    for cp in copies:
        cp.wait()


def both(m, l):
    count = m.shape[0]
    lane = lax.broadcasted_iota(jnp.int32, (count, HD), 1)
    return jnp.where(lane == 0, m, l)


def softmax_once(pieces, twice=False):
    m = functools.reduce(jnp.maximum, [jnp.max(s, axis=1, keepdims=True) for s, _ in pieces])
    l = 0.0
    acc = 0.0
    for s, v in pieces:
        p = jnp.exp2((s - m) * EXP_SCALE)
        if twice:
            col = lax.broadcasted_iota(jnp.int32, (1, s.shape[1]), 1)
            p = jnp.concatenate([p[:128] * jnp.where(col < 128, 2.0, 1.0), p[128:]], axis=0)
        l = l + jnp.sum(p, axis=1, keepdims=True)
        acc = acc + dot_n(p.astype(BF16), v)
    return m, l, acc


def combine(terms):
    top = functools.reduce(jnp.maximum, [t[0] for t in terms])
    length = 0.0
    total = 0.0
    for m, l, acc in terms:
        w = jnp.exp2((m - top) * EXP_SCALE)
        length = length + l * w
        total = total + acc * w
    return top, length, total


def term(acc, ml, at):
    pair = ml[at, :]
    return pair[:, 0:1], pair[:, 1:2], acc[at, :]


def near_kernel(
    raw, qm, msg, cache_h, near_h, acc_h, ml_h, cache,
    acc_s, ml_s, near_o, acc_o, ml_o, sem, out_sem,
):
    rows = raw.shape[1]
    step = 256
    fetch = pltpu.make_async_copy(cache_h, cache, sem.at[2])
    fetch.start()
    copies = []
    inner = lax.div(lax.rem(head_id(), 16), 4)

    def order(dims, dim):
        a = lax.broadcasted_iota(jnp.int32, dims, dim)
        return 4 * (a & 127) + ((lax.shift_right_logical(a, 7) + inner) & 3)

    mine = pl.ds(0, 512)
    s = dot_t(qm[...], msg[mine, pl.ds(0, HD)])
    s = jnp.where(order((1, 512), 1) <= order((512, 1), 0), s, NEG)
    m, l, acc = softmax_once([(s, msg[mine, pl.ds(HD, HD)])], True)
    acc_o[...] = acc
    ml_o[...] = both(m, l)
    tri = lax.broadcasted_iota(jnp.int32, (step, step), 1) <= lax.broadcasted_iota(
        jnp.int32, (step, step), 0
    )
    for b in range(rows // step):
        at = pl.ds(step * b, step)
        q = raw[0, at, :]
        parts = [(jnp.where(tri, dot_t(q, raw[1, at, :]), NEG), raw[2, at, :])]
        if b:
            before = pl.ds(0, step * b)
            parts.append((dot_t(q, raw[1, before, :]), raw[2, before, :]))
        m, l, acc = softmax_once(parts)
        near_o[at, :] = (acc / l).astype(BF16)
        cp = pltpu.make_async_copy(near_o.at[at], near_h.at[at], out_sem.at[b])
        cp.start()
        copies.append(cp)
        acc_s[at, :] = acc
        ml_s[at, :] = both(m, l)
    for c in range(4):
        at = pl.ds(128 * c, 128)
        pick = pl.ds(class_residue(c), 128, stride=16)
        m, l, acc = combine([term(acc_s, ml_s, pick), term(acc_o, ml_o, at)])
        acc_o[at, :] = acc
        ml_o[at, :] = both(m, l)
    for i, (src, dst) in enumerate(((acc_o, acc_h), (ml_o, ml_h))):
        cp = pltpu.make_async_copy(src, dst, sem.at[i])
        cp.start()
        copies.append(cp)
    for cp in copies:
        cp.wait()
    fetch.wait()


def pack(rows_m, rows_l):
    count = rows_m.shape[0]
    lane = lax.broadcasted_iota(jnp.int32, (count, HD), 1)
    st = jnp.zeros((count, HD), F32)
    for at, piece in enumerate(pieces(rows_m) + pieces(rows_l)):
        st = jnp.where(lane == at, piece, st)
    blocks = [st[128 * i : 128 * i + 128].T[:8] for i in range(count // 128)]
    if len(blocks) % 2:
        blocks.append(jnp.zeros((8, HD), F32))
    return jnp.concatenate(blocks, axis=0).astype(BF16)


def unpack(rows):
    st = rows.astype(F32)
    m = st[0:1] + st[1:2] + st[2:3]
    l = st[3:4] + st[4:5] + st[5:6]
    turned = jnp.concatenate([m, l, jnp.zeros((126, HD), F32)], axis=0).T
    return turned[:, 0:1], turned[:, 1:2]


def share_kernel(
    qm, msg, got1, got2, got3, col1, col2, col3, acc_h, ml_h,
    acc_o, ml_o, back1, back2, back3,
    acc_n, ml_n, acc_m, ml_m, acc_2, ml_2, acc_f, ml_f, qf, kf, sem,
):
    z = lax.axis_index("seq")
    local = lax.rem(z, 4)
    group = lax.div(z, 4)
    load_acc = pltpu.make_async_copy(acc_h, acc_n, sem.at[0])
    load_ml = pltpu.make_async_copy(ml_h, ml_n, sem.at[1])
    load_acc.start()
    load_ml.start()
    one = pl.ds(0, 512)
    head = pl.ds(0, 128)
    tail = pl.ds(128, 384)
    keys, values = pl.ds(0, HD), pl.ds(HD, HD)

    def fill(valid, acc_r, ml_r, compute):
        @pl.when(valid)
        def _():
            m, l, acc = compute()
            acc_r[...] = acc
            ml_r[...] = both(m, l)

        @pl.when(jnp.logical_not(valid))
        def _():
            acc_r[...] = jnp.zeros((512, HD), F32)
            ml_r[...] = both(jnp.full((512, 1), NEG, F32), jnp.zeros((512, 1), F32))

    def other_pair():
        q = got2[...]
        return softmax_once(
            [
                (dot_t(q, msg[one, keys]), msg[one, values]),
                (dot_t(q, got1[one, keys]), got1[one, values]),
            ],
            True,
        )

    def own_pair():
        return softmax_once([(dot_t(qm[...], got1[one, keys]), got1[one, values])], True)

    def far_level():
        half = pl.ds(512, 64)
        qf[pl.ds(0, 128), :] = qm[head, :]
        qf[pl.ds(128, 128), :] = got2[head, :]
        qf[pl.ds(256, 64), :] = got1[half, keys]
        qf[pl.ds(320, 64), :] = got1[half, values]
        qf[pl.ds(384, 128), :] = got3[...]
        for i, col in enumerate((col1, col2, col3)):
            kf[pl.ds(128 * i, 128), :] = col[...]
        s = dot_t(qf[...], kf[:, keys])
        at = lax.broadcasted_iota(jnp.int32, (1, 384), 1)
        return softmax_once([(jnp.where(at < 128 * group, s, NEG), kf[:, values])])

    fill(local < 2, acc_2, ml_2, other_pair)
    fill((local & 1) == 1, acc_m, ml_m, own_pair)
    fill(group > 0, acc_f, ml_f, far_level)

    def give(out, terms, rows):
        m, l, acc = combine(terms)
        out[rows, :] = (acc / jnp.where(l > 0.0, l, 1.0)).astype(BF16)
        return m, l

    far2 = term(acc_f, ml_f, pl.ds(128, 128))
    m_a, l_a = give(back2, [term(acc_2, ml_2, head), far2], head)
    m_b, l_b = give(back2, [term(acc_2, ml_2, tail)], tail)
    back2[pl.ds(512, 32), :] = pack(
        jnp.concatenate([m_a, m_b], axis=0), jnp.concatenate([l_a, l_b], axis=0)
    )
    for out, first in ((back1, 256), (back3, 384)):
        m, l = give(out, [term(acc_f, ml_f, pl.ds(first, 128))], head)
        out[pl.ds(128, 16), :] = pack(m, l)
    load_acc.wait()
    load_ml.wait()
    for at in (head, tail):
        terms = [term(acc_n, ml_n, at), term(acc_m, ml_m, at)]
        if at is head:
            terms.append(term(acc_f, ml_f, head))
        m, l, acc = combine(terms)
        acc_n[at, :] = acc
        ml_n[at, :] = both(m, l)
    save_acc = pltpu.make_async_copy(acc_n, acc_o, sem.at[0])
    save_ml = pltpu.make_async_copy(ml_n, ml_o, sem.at[1])
    save_acc.start()
    save_ml.start()
    save_acc.wait()
    save_ml.wait()


def merge_kernel(near_h, acc_h, ml_h, back1, back2, back3, out, near, acc, ml, wide, sem):
    copies = [
        pltpu.make_async_copy(src, dst, sem.at[i])
        for i, (src, dst) in enumerate(((near_h, near), (acc_h, acc), (ml_h, ml)))
    ]
    for cp in copies:
        cp.start()
    for cp in copies:
        cp.wait()
    wide[...] = near[...].astype(F32)
    for c in range(4):
        at = pl.ds(128 * c, 128)
        terms = [(ml[at, :][:, 0:1], ml[at, :][:, 1:2], acc[at, :])]
        for part, rows, stat in ((back2, 128 * c, 512 + 8 * c), (back1, 0, 128), (back3, 0, 128)):
            if c and part is not back2:
                continue
            pm, plen = unpack(part[pl.ds(stat // 16 * 16, 16), :][stat % 16 : stat % 16 + 8])
            terms.append((pm, plen, part[pl.ds(rows, 128), :].astype(F32) * plen))
        top = functools.reduce(jnp.maximum, [t[0] for t in terms])
        total = 0.0
        length = 0.0
        for tm, tl, ta in terms:
            w = jnp.exp2((tm - top) * EXP_SCALE)
            length = length + tl * w
            total = total + ta * w
        wide[pl.ds(class_residue(c), 128, stride=16), :] = total / length
    out[...] = wide[...].astype(BF16)


def pieces(x):
    hi = x.astype(BF16).astype(F32)
    rest = x - hi
    mid = rest.astype(BF16).astype(F32)
    return hi, mid, (rest - mid).astype(BF16).astype(F32)


def cache_kernel(own, lens, arr, cache, out, o_s, st_s):
    z = lax.axis_index("seq")
    me = lax.axis_index("req")
    per = cache.shape[2]
    width = cache.shape[3]
    diag = lax.shift_right_logical(
        lax.broadcasted_iota(jnp.int32, (16, width), 1), 7
    ) == lax.shift_right_logical(lax.broadcasted_iota(jnp.int32, (16, width), 0), 1)
    token = lax.broadcasted_iota(jnp.int32, (16, 16), 0) & 1
    new_col = lax.broadcasted_iota(jnp.int32, (16, 16), 1)
    new_ok = (new_col <= token) & (z == 0)
    col = z * per + lax.broadcasted_iota(jnp.int32, (16, per), 1)
    row_head = lax.shift_right_logical(lax.broadcasted_iota(jnp.int32, (16, HD), 0), 1)
    lane = lax.broadcasted_iota(jnp.int32, (16, HD), 1)
    pad = jnp.zeros((14, width), F32)
    for k in range(4):
        grp, rank = rank_in_block(own, 4 * me, k)
        row = 2 * grp + rank
        q = arr[row, 0].astype(F32)
        qd = jnp.where(diag, jnp.concatenate([q] * 8, axis=0), 0.0).astype(BF16)
        kn = jnp.concatenate([arr[row, 1].astype(F32), pad], axis=0).astype(BF16)
        vn = jnp.concatenate([arr[row, 2].astype(F32), pad], axis=0).astype(BF16)
        c_ok = col < lens[4 * me + k]
        s_c = jnp.where(c_ok, dot_t(qd, cache[k, 0]), NEG)
        s_n = jnp.where(new_ok, dot_t(qd, kn), NEG)
        m = jnp.maximum(
            jnp.max(s_c, axis=1, keepdims=True), jnp.max(s_n, axis=1, keepdims=True)
        )
        p_c = jnp.where(c_ok, jnp.exp2((s_c - m) * EXP_SCALE), 0.0)
        p_n = jnp.where(new_ok, jnp.exp2((s_n - m) * EXP_SCALE), 0.0)
        l = jnp.sum(p_c, axis=1, keepdims=True) + jnp.sum(p_n, axis=1, keepdims=True)
        full = dot_n(p_c.astype(BF16), cache[k, 1]) + dot_n(p_n.astype(BF16), vn)
        o = jnp.zeros((16, HD), F32)
        for h in range(8):
            o = jnp.where(row_head == h, full[:, HD * h : HD * (h + 1)], o)
        o = o / jnp.where(l > 0.0, l, 1.0)
        st = jnp.zeros((16, HD), F32)
        for at, piece in enumerate(pieces(m) + pieces(l)):
            st = jnp.where(lane == at, piece, st)
        for h in range(8):
            o_s[pl.ds(8 * h + 2 * k, 2), :] = o[2 * h : 2 * h + 2]
            st_s[pl.ds(8 * h + 2 * k, 2), :] = st[2 * h : 2 * h + 2]
    values = o_s[...].astype(BF16)
    turned = st_s[...].T
    stats = jnp.concatenate([turned[:16, :], jnp.zeros((16, 64), F32)], axis=1).astype(BF16)
    for t in range(out.shape[0]):
        out[t, pl.ds(0, 64), :] = values
        out[t, pl.ds(64, 16), :] = stats


def project_kernel(own, got, weight, out):
    me = lax.axis_index("req")
    count = got.shape[0]
    ms, ls = [], []
    for t in range(count):
        st = got[t, pl.ds(64, 16), :].astype(F32)
        ms.append(st[0:1] + st[1:2] + st[2:3])
        ls.append(st[3:4] + st[4:5] + st[5:6])
    m = jnp.concatenate(ms, axis=0)
    l = jnp.concatenate(ls, axis=0)
    share = jnp.exp2((m - jnp.max(m, axis=0, keepdims=True)) * EXP_SCALE) * l
    share = share / jnp.sum(share, axis=0, keepdims=True)
    share = jnp.concatenate([share, jnp.zeros((128 - count, HD), F32)], axis=0).T
    total = jnp.zeros((64, HD), F32)
    for t in range(count):
        total = total + share[:64, t : t + 1] * got[t, pl.ds(0, 64), :].astype(F32)
    rows = jnp.concatenate([total[8 * h : 8 * h + 8] for h in range(8)], axis=1)
    y = dot_n(rows.astype(BF16), weight[...])
    out[...] = jnp.zeros(out.shape, BF16)
    seats = [rank_in_block(own, 4 * me, k) for k in range(4)]
    for h in range(4):
        cols = slice(64 * h, 64 * h + 64)
        lines = [
            jnp.concatenate([y[2 * k : 2 * k + 1, cols], y[2 * k + 1 : 2 * k + 2, cols]], axis=1)
            for k in range(4)
        ]
        for grp, _ in seats:
            pair = [jnp.zeros((1, HD), F32)] * 2
            for (other, rank), line in zip(seats, lines):
                for r in range(2):
                    pair[r] = jnp.where((other == grp) & (rank == r), line, pair[r])
            out[8 * h + grp] = jnp.concatenate(pair, axis=0).astype(BF16)


def settle_kernel(own, got, out):
    me = lax.axis_index("req")
    total = got[pl.ds(0, 8)].astype(F32)
    for h in range(1, 4):
        total = total + got[pl.ds(8 * h, 8)].astype(F32)
    out[...] = jnp.zeros(out.shape, BF16)
    for b in range(8):
        first = total[b]
        for k in range(4):
            slot = own[4 * b + k]
            grp, rank = rank_in_block(own, 4 * b, k)

            @pl.when(grp == me)
            def _(first=first, slot=slot, rank=rank):
                row = jnp.where(rank == 0, first[0:1], first[1:2])
                out[slot & 15] = jnp.concatenate([row[:, :64], row[:, 64:]], axis=0).astype(BF16)


def shape(dims, dtype=BF16):
    return jax.ShapeDtypeStruct(dims, dtype)


def staged(pre_qkv, cache_kv, dec_new, out_weight, owner_slot, prompt_lengths):
    qkv = jnp.swapaxes(pre_qkv, 0, 1)
    raw, sent, qm, ask, msg, far = call(
        start_kernel,
        (
            shape((3, 2048, HD)),
            shape(dec_new.shape),
            shape((512, HD)),
            shape((128, HD)),
            shape((576, 2 * HD)),
            shape((128, 2 * HD)),
        ),
        (far_memory(owner_slot), far_memory(dec_new), far_memory(qkv)),
        [hspec(), hspec(), hspec()],
        [
            SMEM((32,), jnp.int32),
            VMEM((2048, HD), F32),
            pltpu.SemaphoreType.DMA((16,)),
            pltpu.SemaphoreType.DMA((3,)),
            pltpu.SemaphoreType.DMA,
        ],
        nbytes=4000000,
    )
    arrived = lax.all_to_all(sent, "req", 0, 0, tiled=True)

    def swap(x, bits):
        return lax.ppermute(x, "seq", [(i, i ^ bits) for i in range(16)])

    def relay(x, first):
        return lax.ppermute(x, "seq", [(i, i + 4) for i in range(first, 12)])

    col1 = relay(far, 0)
    got3 = swap(ask, 3)
    got2 = swap(qm, 2)
    got1 = swap(msg, 1)
    col2 = relay(col1, 4)
    state = [pltpu.HBM((512, HD), F32)] * 2
    near_o, acc, ml, cache = call(
        near_kernel,
        (pltpu.HBM((2048, HD), BF16), *state, shape(cache_kv.shape)),
        (raw, qm, msg, far_memory(cache_kv)),
        [vspec(), vspec(), vspec(), hspec()],
        [
            VMEM((2048, HD), F32),
            VMEM((2048, HD), F32),
            VMEM((2048, HD), BF16),
            VMEM((512, HD), F32),
            VMEM((512, HD), F32),
            pltpu.SemaphoreType.DMA((8,)),
            pltpu.SemaphoreType.DMA((8,)),
        ],
        flops=2 * 10**9,
        nbytes=3000000,
        trans=2 * 10**6,
        outs=[hspec(), hspec(), hspec(), vspec()],
    )
    partial = call(
        cache_kernel,
        shape((16, 80, HD)),
        (owner_slot, prompt_lengths, arrived, cache),
        [sspec(), sspec(), vspec(), vspec()],
        [VMEM((64, HD), F32), VMEM((64, HD), F32)],
        flops=10**8,
        nbytes=2000000,
    )
    parts = lax.all_to_all(partial, "seq", 0, 0, tiled=True)
    col3 = relay(col2, 8)
    acc, ml, back1, back2, back3 = call(
        share_kernel,
        (*state, shape((144, HD)), shape((544, HD)), shape((144, HD))),
        (qm, msg, got1, got2, got3, col1, col2, col3, far_memory(acc), far_memory(ml)),
        [vspec()] * 8 + [hspec()] * 2,
        [VMEM((512, HD), F32)] * 8
        + [VMEM((512, HD), BF16), VMEM((384, 2 * HD), BF16), pltpu.SemaphoreType.DMA((2,))],
        flops=10**9,
        nbytes=4000000,
        trans=10**6,
        outs=[hspec()] * 2 + [vspec()] * 3,
    )
    back1 = swap(back1, 1)
    back3 = swap(back3, 3)
    back2 = swap(back2, 2)
    answers = call(
        project_kernel,
        shape((32, 2, HD)),
        (owner_slot, parts, out_weight),
        [sspec(), vspec(), vspec()],
        flops=10**7,
        nbytes=1000000,
    )
    results = lax.all_to_all(answers, ("head", "req"), 0, 0, tiled=True)
    prefill_out = call(
        merge_kernel,
        shape((2048, HD)),
        (far_memory(near_o), far_memory(acc), far_memory(ml), back1, back2, back3),
        [hspec()] * 3 + [vspec()] * 3,
        [
            VMEM((2048, HD), BF16),
            VMEM((512, HD), F32),
            VMEM((512, HD), F32),
            VMEM((2048, HD), F32),
            pltpu.SemaphoreType.DMA((3,)),
        ],
        flops=10**8,
        nbytes=4000000,
    )
    decode_out = call(
        settle_kernel,
        shape((16, 2, 64)),
        (owner_slot, results),
        [sspec(), vspec()],
        nbytes=100000,
    )
    return prefill_out, decode_out


def solution(mesh):
    return jax.shard_map(
        staged,
        mesh=mesh,
        in_specs=(
            P("seq", None, ("head", "req")),
            P("req", None, "seq", "head"),
            P("req", None, None, "head"),
            P("head", "seq"),
            P(),
            P(),
        ),
        out_specs=(P("seq", ("head", "req")), P("req", None, ("seq", "head"))),
        check_vma=False,
    )
```

```python
import functools
import math

import jax
import jax.numpy as jnp
from jax import lax
from jax.experimental import pallas as pl
from jax.experimental.pallas import tpu as pltpu
from jax.sharding import PartitionSpec as P

HD = 128
NEG = -1e30
EXP_SCALE = HD**-0.5 * math.log2(math.e)
F32 = jnp.float32
BF16 = jnp.bfloat16

VMEM = pltpu.VMEM
SMEM = pltpu.SMEM


def vspec():
    return pl.BlockSpec(memory_space=pltpu.VMEM)


def far_memory(x):
    return pltpu.with_memory_space_constraint(x, pltpu.HBM)


def hspec():
    return pl.BlockSpec(memory_space=pltpu.HBM)


def sspec():
    return pl.BlockSpec(memory_space=pltpu.SMEM)


def dot_t(a, b):
    return lax.dot_general(a, b, (((1,), (1,)), ((), ())), preferred_element_type=F32)


def dot_n(a, b):
    return lax.dot_general(a, b, (((1,), (0,)), ((), ())), preferred_element_type=F32)


def call(body, out_shape, ins, specs, scratch=(), vmem=24, flops=0, nbytes=0, trans=0, outs=None):
    single = not isinstance(out_shape, (tuple, list))
    return pl.pallas_call(
        body,
        out_shape=out_shape,
        in_specs=specs,
        out_specs=vspec() if single else tuple(outs or [vspec() for _ in out_shape]),
        scratch_shapes=list(scratch),
        compiler_params=pltpu.CompilerParams(vmem_limit_bytes=vmem * 1024 * 1024),
        cost_estimate=pl.CostEstimate(flops=flops, bytes_accessed=nbytes, transcendentals=trans),
    )(*ins)


def head_id():
    return lax.axis_index("head") * lax.axis_size("req") + lax.axis_index("req")


def class_residue(c):
    j = head_id()
    r4 = lax.rem(j, 4)
    inner = lax.div(lax.rem(j, 16), 4)
    return 4 * lax.rem(c + inner, 4) + r4


def rank_in_block(own, first, k):
    grp = lax.shift_right_logical(own[first + k], 4)
    rank = jnp.int32(0)
    for e in range(k):
        rank += (lax.shift_right_logical(own[first + e], 4) == grp).astype(jnp.int32)
    return grp, rank


def start_kernel(
    own_h, dec, qkv, raw, sent, qm, ask, msg, far, own, wide, sem, part_sem, own_sem
):
    own_copy = pltpu.make_async_copy(own_h, own, own_sem)
    own_copy.start()
    me = lax.axis_index("req")
    rows = qkv.shape[1]
    parts = []
    for part in range(3):
        cp = pltpu.make_async_copy(qkv.at[part], raw.at[part], part_sem.at[part])
        cp.start()
        parts.append(cp)
    copies = []
    own_copy.wait()
    for b in range(8):
        src = [jnp.int32(0), jnp.int32(0)]
        for k in range(4):
            slot = own[4 * b + k]
            grp, rank = rank_in_block(own, 4 * b, k)
            mine = grp == me
            for r in range(2):
                src[r] = jnp.where(mine & (rank == r), slot & 15, src[r])
        for r in range(2):
            cp = pltpu.make_async_copy(dec.at[src[r]], sent.at[2 * b + r], sem.at[2 * b + r])
            cp.start()
            copies.append(cp)
    for part in range(3):
        parts[part].wait()
        wide[...] = raw[part].astype(F32)
        for c in range(4):
            start = class_residue(c)
            got = wide[pl.ds(start, rows // 16, stride=16), :].astype(BF16)
            at = pl.ds(128 * c, 128)
            if part == 0:
                qm[at, :] = got
                if c == 0:
                    ask[...] = got
                    msg[pl.ds(512, 64), pl.ds(0, HD)] = got[:64]
                    msg[pl.ds(512, 64), pl.ds(HD, HD)] = got[64:]
            else:
                lanes = pl.ds(HD * (part - 1), HD)
                msg[at, lanes] = got
                if c == 0:
                    far[:, lanes] = got
    for cp in copies:
        cp.wait()


def both(m, l):
    count = m.shape[0]
    lane = lax.broadcasted_iota(jnp.int32, (count, HD), 1)
    return jnp.where(lane == 0, m, l)


def softmax_once(pieces, twice=False):
    m = functools.reduce(jnp.maximum, [jnp.max(s, axis=1, keepdims=True) for s, _ in pieces])
    l = 0.0
    acc = 0.0
    for s, v in pieces:
        p = jnp.exp2((s - m) * EXP_SCALE)
        if twice:
            col = lax.broadcasted_iota(jnp.int32, (1, s.shape[1]), 1)
            p = jnp.concatenate([p[:128] * jnp.where(col < 128, 2.0, 1.0), p[128:]], axis=0)
        l = l + jnp.sum(p, axis=1, keepdims=True)
        acc = acc + dot_n(p.astype(BF16), v)
    return m, l, acc


def combine(terms):
    top = functools.reduce(jnp.maximum, [t[0] for t in terms])
    length = 0.0
    total = 0.0
    for m, l, acc in terms:
        w = jnp.exp2((m - top) * EXP_SCALE)
        length = length + l * w
        total = total + acc * w
    return top, length, total


def term(acc, ml, at):
    pair = ml[at, :]
    return pair[:, 0:1], pair[:, 1:2], acc[at, :]


def near_kernel(
    raw, qm, msg, cache_h, near_h, acc_h, ml_h, cache,
    acc_s, ml_s, near_o, acc_o, ml_o, sem, out_sem,
):
    rows = raw.shape[1]
    step = 256
    fetch = pltpu.make_async_copy(cache_h, cache, sem.at[2])
    fetch.start()
    copies = []
    inner = lax.div(lax.rem(head_id(), 16), 4)

    def order(dims, dim):
        a = lax.broadcasted_iota(jnp.int32, dims, dim)
        return 4 * (a & 127) + ((lax.shift_right_logical(a, 7) + inner) & 3)

    mine = pl.ds(0, 512)
    s = dot_t(qm[...], msg[mine, pl.ds(0, HD)])
    s = jnp.where(order((1, 512), 1) <= order((512, 1), 0), s, NEG)
    m, l, acc = softmax_once([(s, msg[mine, pl.ds(HD, HD)])], True)
    acc_o[...] = acc
    ml_o[...] = both(m, l)
    tri = lax.broadcasted_iota(jnp.int32, (step, step), 1) <= lax.broadcasted_iota(
        jnp.int32, (step, step), 0
    )
    for b in range(rows // step):
        at = pl.ds(step * b, step)
        q = raw[0, at, :]
        parts = [(jnp.where(tri, dot_t(q, raw[1, at, :]), NEG), raw[2, at, :])]
        if b:
            before = pl.ds(0, step * b)
            parts.append((dot_t(q, raw[1, before, :]), raw[2, before, :]))
        m, l, acc = softmax_once(parts)
        near_o[at, :] = (acc / l).astype(BF16)
        cp = pltpu.make_async_copy(near_o.at[at], near_h.at[at], out_sem.at[b])
        cp.start()
        copies.append(cp)
        acc_s[at, :] = acc
        ml_s[at, :] = both(m, l)
    for c in range(4):
        at = pl.ds(128 * c, 128)
        pick = pl.ds(class_residue(c), 128, stride=16)
        m, l, acc = combine([term(acc_s, ml_s, pick), term(acc_o, ml_o, at)])
        acc_o[at, :] = acc
        ml_o[at, :] = both(m, l)
    for i, (src, dst) in enumerate(((acc_o, acc_h), (ml_o, ml_h))):
        cp = pltpu.make_async_copy(src, dst, sem.at[i])
        cp.start()
        copies.append(cp)
    for cp in copies:
        cp.wait()
    fetch.wait()


def pack(rows_m, rows_l):
    count = rows_m.shape[0]
    lane = lax.broadcasted_iota(jnp.int32, (count, HD), 1)
    st = jnp.zeros((count, HD), F32)
    for at, piece in enumerate(pieces(rows_m) + pieces(rows_l)):
        st = jnp.where(lane == at, piece, st)
    blocks = [st[128 * i : 128 * i + 128].T[:8] for i in range(count // 128)]
    if len(blocks) % 2:
        blocks.append(jnp.zeros((8, HD), F32))
    return jnp.concatenate(blocks, axis=0).astype(BF16)


def unpack(rows):
    st = rows.astype(F32)
    m = st[0:1] + st[1:2] + st[2:3]
    l = st[3:4] + st[4:5] + st[5:6]
    turned = jnp.concatenate([m, l, jnp.zeros((126, HD), F32)], axis=0).T
    return turned[:, 0:1], turned[:, 1:2]


def share_kernel(
    qm, msg, got1, got2, got3, col1, col2, col3, acc_h, ml_h,
    acc_o, ml_o, back1, back2, back3,
    acc_n, ml_n, acc_m, ml_m, acc_2, ml_2, acc_f, ml_f, qf, kf, sem,
):
    z = lax.axis_index("seq")
    local = lax.rem(z, 4)
    group = lax.div(z, 4)
    load_acc = pltpu.make_async_copy(acc_h, acc_n, sem.at[0])
    load_ml = pltpu.make_async_copy(ml_h, ml_n, sem.at[1])
    load_acc.start()
    load_ml.start()
    one = pl.ds(0, 512)
    head = pl.ds(0, 128)
    tail = pl.ds(128, 384)
    keys, values = pl.ds(0, HD), pl.ds(HD, HD)

    def fill(valid, acc_r, ml_r, compute):
        @pl.when(valid)
        def _():
            m, l, acc = compute()
            acc_r[...] = acc
            ml_r[...] = both(m, l)

        @pl.when(jnp.logical_not(valid))
        def _():
            acc_r[...] = jnp.zeros((512, HD), F32)
            ml_r[...] = both(jnp.full((512, 1), NEG, F32), jnp.zeros((512, 1), F32))

    def other_pair():
        q = got2[...]
        return softmax_once(
            [
                (dot_t(q, msg[one, keys]), msg[one, values]),
                (dot_t(q, got1[one, keys]), got1[one, values]),
            ],
            True,
        )

    def own_pair():
        return softmax_once([(dot_t(qm[...], got1[one, keys]), got1[one, values])], True)

    def far_level():
        half = pl.ds(512, 64)
        qf[pl.ds(0, 128), :] = qm[head, :]
        qf[pl.ds(128, 128), :] = got2[head, :]
        qf[pl.ds(256, 64), :] = got1[half, keys]
        qf[pl.ds(320, 64), :] = got1[half, values]
        qf[pl.ds(384, 128), :] = got3[...]
        for i, col in enumerate((col1, col2, col3)):
            kf[pl.ds(128 * i, 128), :] = col[...]
        s = dot_t(qf[...], kf[:, keys])
        at = lax.broadcasted_iota(jnp.int32, (1, 384), 1)
        return softmax_once([(jnp.where(at < 128 * group, s, NEG), kf[:, values])])

    fill(local < 2, acc_2, ml_2, other_pair)
    fill((local & 1) == 1, acc_m, ml_m, own_pair)
    fill(group > 0, acc_f, ml_f, far_level)

    def give(out, terms, rows):
        m, l, acc = combine(terms)
        out[rows, :] = (acc / jnp.where(l > 0.0, l, 1.0)).astype(BF16)
        return m, l

    far2 = term(acc_f, ml_f, pl.ds(128, 128))
    m_a, l_a = give(back2, [term(acc_2, ml_2, head), far2], head)
    m_b, l_b = give(back2, [term(acc_2, ml_2, tail)], tail)
    back2[pl.ds(512, 32), :] = pack(
        jnp.concatenate([m_a, m_b], axis=0), jnp.concatenate([l_a, l_b], axis=0)
    )
    for out, first in ((back1, 256), (back3, 384)):
        m, l = give(out, [term(acc_f, ml_f, pl.ds(first, 128))], head)
        out[pl.ds(128, 16), :] = pack(m, l)
    load_acc.wait()
    load_ml.wait()
    for at in (head, tail):
        terms = [term(acc_n, ml_n, at), term(acc_m, ml_m, at)]
        if at is head:
            terms.append(term(acc_f, ml_f, head))
        m, l, acc = combine(terms)
        acc_n[at, :] = acc
        ml_n[at, :] = both(m, l)
    save_acc = pltpu.make_async_copy(acc_n, acc_o, sem.at[0])
    save_ml = pltpu.make_async_copy(ml_n, ml_o, sem.at[1])
    save_acc.start()
    save_ml.start()
    save_acc.wait()
    save_ml.wait()


def merge_kernel(near_h, acc_h, ml_h, back1, back2, back3, out, near, acc, ml, wide, sem):
    copies = [
        pltpu.make_async_copy(src, dst, sem.at[i])
        for i, (src, dst) in enumerate(((near_h, near), (acc_h, acc), (ml_h, ml)))
    ]
    for cp in copies:
        cp.start()
    for cp in copies:
        cp.wait()
    wide[...] = near[...].astype(F32)
    for c in range(4):
        at = pl.ds(128 * c, 128)
        terms = [(ml[at, :][:, 0:1], ml[at, :][:, 1:2], acc[at, :])]
        for part, rows, stat in ((back2, 128 * c, 512 + 8 * c), (back1, 0, 128), (back3, 0, 128)):
            if c and part is not back2:
                continue
            pm, plen = unpack(part[pl.ds(stat // 16 * 16, 16), :][stat % 16 : stat % 16 + 8])
            terms.append((pm, plen, part[pl.ds(rows, 128), :].astype(F32) * plen))
        top = functools.reduce(jnp.maximum, [t[0] for t in terms])
        total = 0.0
        length = 0.0
        for tm, tl, ta in terms:
            w = jnp.exp2((tm - top) * EXP_SCALE)
            length = length + tl * w
            total = total + ta * w
        wide[pl.ds(class_residue(c), 128, stride=16), :] = total / length
    out[...] = wide[...].astype(BF16)


def pieces(x):
    hi = x.astype(BF16).astype(F32)
    rest = x - hi
    mid = rest.astype(BF16).astype(F32)
    return hi, mid, (rest - mid).astype(BF16).astype(F32)


def cache_kernel(own, lens, arr, cache, out, o_s, st_s):
    z = lax.axis_index("seq")
    me = lax.axis_index("req")
    per = cache.shape[2]
    width = cache.shape[3]
    diag = lax.shift_right_logical(
        lax.broadcasted_iota(jnp.int32, (16, width), 1), 7
    ) == lax.shift_right_logical(lax.broadcasted_iota(jnp.int32, (16, width), 0), 1)
    token = lax.broadcasted_iota(jnp.int32, (16, 16), 0) & 1
    new_col = lax.broadcasted_iota(jnp.int32, (16, 16), 1)
    new_ok = (new_col <= token) & (z == 0)
    col = z * per + lax.broadcasted_iota(jnp.int32, (16, per), 1)
    row_head = lax.shift_right_logical(lax.broadcasted_iota(jnp.int32, (16, HD), 0), 1)
    lane = lax.broadcasted_iota(jnp.int32, (16, HD), 1)
    pad = jnp.zeros((14, width), F32)
    for k in range(4):
        grp, rank = rank_in_block(own, 4 * me, k)
        row = 2 * grp + rank
        q = arr[row, 0].astype(F32)
        qd = jnp.where(diag, jnp.concatenate([q] * 8, axis=0), 0.0).astype(BF16)
        kn = jnp.concatenate([arr[row, 1].astype(F32), pad], axis=0).astype(BF16)
        vn = jnp.concatenate([arr[row, 2].astype(F32), pad], axis=0).astype(BF16)
        c_ok = col < lens[4 * me + k]
        s_c = jnp.where(c_ok, dot_t(qd, cache[k, 0]), NEG)
        s_n = jnp.where(new_ok, dot_t(qd, kn), NEG)
        m = jnp.maximum(
            jnp.max(s_c, axis=1, keepdims=True), jnp.max(s_n, axis=1, keepdims=True)
        )
        p_c = jnp.where(c_ok, jnp.exp2((s_c - m) * EXP_SCALE), 0.0)
        p_n = jnp.where(new_ok, jnp.exp2((s_n - m) * EXP_SCALE), 0.0)
        l = jnp.sum(p_c, axis=1, keepdims=True) + jnp.sum(p_n, axis=1, keepdims=True)
        full = dot_n(p_c.astype(BF16), cache[k, 1]) + dot_n(p_n.astype(BF16), vn)
        o = jnp.zeros((16, HD), F32)
        for h in range(8):
            o = jnp.where(row_head == h, full[:, HD * h : HD * (h + 1)], o)
        o = o / jnp.where(l > 0.0, l, 1.0)
        st = jnp.zeros((16, HD), F32)
        for at, piece in enumerate(pieces(m) + pieces(l)):
            st = jnp.where(lane == at, piece, st)
        for h in range(8):
            o_s[pl.ds(8 * h + 2 * k, 2), :] = o[2 * h : 2 * h + 2]
            st_s[pl.ds(8 * h + 2 * k, 2), :] = st[2 * h : 2 * h + 2]
    values = o_s[...].astype(BF16)
    turned = st_s[...].T
    stats = jnp.concatenate([turned[:8, :], jnp.zeros((8, 64), F32)], axis=1).astype(BF16)
    for t in range(out.shape[0]):
        out[t, pl.ds(0, 64), :] = values
        out[t, pl.ds(64, 8), :] = stats


def project_kernel(own, got, weight, out):
    me = lax.axis_index("req")
    count = got.shape[0]
    ms, ls = [], []
    for t in range(count):
        st = got[t, pl.ds(64, 8), :].astype(F32)
        ms.append(st[0:1] + st[1:2] + st[2:3])
        ls.append(st[3:4] + st[4:5] + st[5:6])
    m = jnp.concatenate(ms, axis=0)
    l = jnp.concatenate(ls, axis=0)
    share = jnp.exp2((m - jnp.max(m, axis=0, keepdims=True)) * EXP_SCALE) * l
    share = share / jnp.sum(share, axis=0, keepdims=True)
    share = jnp.concatenate([share, jnp.zeros((128 - count, HD), F32)], axis=0).T
    total = jnp.zeros((64, HD), F32)
    for t in range(count):
        total = total + share[:64, t : t + 1] * got[t, pl.ds(0, 64), :].astype(F32)
    rows = jnp.concatenate([total[8 * h : 8 * h + 8] for h in range(8)], axis=1)
    y = dot_n(rows.astype(BF16), weight[...])
    out[...] = jnp.zeros(out.shape, BF16)
    seats = [rank_in_block(own, 4 * me, k) for k in range(4)]
    for h in range(4):
        cols = slice(64 * h, 64 * h + 64)
        lines = [
            jnp.concatenate([y[2 * k : 2 * k + 1, cols], y[2 * k + 1 : 2 * k + 2, cols]], axis=1)
            for k in range(4)
        ]
        for grp, _ in seats:
            pair = [jnp.zeros((1, HD), F32)] * 2
            for (other, rank), line in zip(seats, lines):
                for r in range(2):
                    pair[r] = jnp.where((other == grp) & (rank == r), line, pair[r])
            out[8 * h + grp] = jnp.concatenate(pair, axis=0).astype(BF16)


def settle_kernel(own, got, out):
    me = lax.axis_index("req")
    total = got[pl.ds(0, 8)].astype(F32)
    for h in range(1, 4):
        total = total + got[pl.ds(8 * h, 8)].astype(F32)
    out[...] = jnp.zeros(out.shape, BF16)
    for b in range(8):
        first = total[b]
        for k in range(4):
            slot = own[4 * b + k]
            grp, rank = rank_in_block(own, 4 * b, k)

            @pl.when(grp == me)
            def _(first=first, slot=slot, rank=rank):
                row = jnp.where(rank == 0, first[0:1], first[1:2])
                out[slot & 15] = jnp.concatenate([row[:, :64], row[:, 64:]], axis=0).astype(BF16)


def shape(dims, dtype=BF16):
    return jax.ShapeDtypeStruct(dims, dtype)


def staged(pre_qkv, cache_kv, dec_new, out_weight, owner_slot, prompt_lengths):
    qkv = jnp.swapaxes(pre_qkv, 0, 1)
    raw, sent, qm, ask, msg, far = call(
        start_kernel,
        (
            shape((3, 2048, HD)),
            shape(dec_new.shape),
            shape((512, HD)),
            shape((128, HD)),
            shape((576, 2 * HD)),
            shape((128, 2 * HD)),
        ),
        (far_memory(owner_slot), far_memory(dec_new), far_memory(qkv)),
        [hspec(), hspec(), hspec()],
        [
            SMEM((32,), jnp.int32),
            VMEM((2048, HD), F32),
            pltpu.SemaphoreType.DMA((16,)),
            pltpu.SemaphoreType.DMA((3,)),
            pltpu.SemaphoreType.DMA,
        ],
        nbytes=4000000,
    )
    arrived = lax.all_to_all(sent, "req", 0, 0, tiled=True)

    def swap(x, bits):
        return lax.ppermute(x, "seq", [(i, i ^ bits) for i in range(16)])

    def relay(x, first, stop, hop):
        return lax.ppermute(x, "seq", [(i, i + hop) for i in range(first, stop)])

    col1 = relay(far, 0, 12, 4)
    col3 = relay(far, 0, 4, 12)
    got3 = swap(ask, 3)
    got2 = swap(qm, 2)
    got1 = swap(msg, 1)
    col2 = relay(col1, 4, 12, 4)
    state = [pltpu.HBM((512, HD), F32)] * 2
    near_o, acc, ml, cache = call(
        near_kernel,
        (pltpu.HBM((2048, HD), BF16), *state, shape(cache_kv.shape)),
        (raw, qm, msg, far_memory(cache_kv)),
        [vspec(), vspec(), vspec(), hspec()],
        [
            VMEM((2048, HD), F32),
            VMEM((2048, HD), F32),
            VMEM((2048, HD), BF16),
            VMEM((512, HD), F32),
            VMEM((512, HD), F32),
            pltpu.SemaphoreType.DMA((8,)),
            pltpu.SemaphoreType.DMA((8,)),
        ],
        flops=2 * 10**9,
        nbytes=3000000,
        trans=2 * 10**6,
        outs=[hspec(), hspec(), hspec(), vspec()],
    )
    partial = call(
        cache_kernel,
        shape((16, 72, HD)),
        (owner_slot, prompt_lengths, arrived, cache),
        [sspec(), sspec(), vspec(), vspec()],
        [VMEM((64, HD), F32), VMEM((64, HD), F32)],
        flops=10**8,
        nbytes=2000000,
    )
    parts = lax.all_to_all(partial, "seq", 0, 0, tiled=True)
    acc, ml, back1, back2, back3 = call(
        share_kernel,
        (*state, shape((144, HD)), shape((544, HD)), shape((144, HD))),
        (qm, msg, got1, got2, got3, col1, col2, col3, far_memory(acc), far_memory(ml)),
        [vspec()] * 8 + [hspec()] * 2,
        [VMEM((512, HD), F32)] * 8
        + [VMEM((512, HD), BF16), VMEM((384, 2 * HD), BF16), pltpu.SemaphoreType.DMA((2,))],
        flops=10**9,
        nbytes=4000000,
        trans=10**6,
        outs=[hspec()] * 2 + [vspec()] * 3,
    )
    back1 = swap(back1, 1)
    back3 = swap(back3, 3)
    back2 = swap(back2, 2)
    answers = call(
        project_kernel,
        shape((32, 2, HD)),
        (owner_slot, parts, out_weight),
        [sspec(), vspec(), vspec()],
        flops=10**7,
        nbytes=1000000,
    )
    results = lax.all_to_all(answers, ("head", "req"), 0, 0, tiled=True)
    prefill_out = call(
        merge_kernel,
        shape((2048, HD)),
        (far_memory(near_o), far_memory(acc), far_memory(ml), back1, back2, back3),
        [hspec()] * 3 + [vspec()] * 3,
        [
            VMEM((2048, HD), BF16),
            VMEM((512, HD), F32),
            VMEM((512, HD), F32),
            VMEM((2048, HD), F32),
            pltpu.SemaphoreType.DMA((3,)),
        ],
        flops=10**8,
        nbytes=4000000,
    )
    decode_out = call(
        settle_kernel,
        shape((16, 2, 64)),
        (owner_slot, results),
        [sspec(), vspec()],
        nbytes=100000,
    )
    return prefill_out, decode_out


def solution(mesh):
    return jax.shard_map(
        staged,
        mesh=mesh,
        in_specs=(
            P("seq", None, ("head", "req")),
            P("req", None, "seq", "head"),
            P("req", None, None, "head"),
            P("head", "seq"),
            P(),
            P(),
        ),
        out_specs=(P("seq", ("head", "req")), P("req", None, ("seq", "head"))),
        check_vma=False,
    )
```

```python
import functools
import math

import jax
import jax.numpy as jnp
from jax import lax
from jax.experimental import pallas as pl
from jax.experimental.pallas import tpu as pltpu
from jax.sharding import PartitionSpec as P

HD = 128
NEG = -1e30
EXP_SCALE = HD**-0.5 * math.log2(math.e)
F32 = jnp.float32
BF16 = jnp.bfloat16

VMEM = pltpu.VMEM
SMEM = pltpu.SMEM


def vspec():
    return pl.BlockSpec(memory_space=pltpu.VMEM)


def far_memory(x):
    return pltpu.with_memory_space_constraint(x, pltpu.HBM)


def hspec():
    return pl.BlockSpec(memory_space=pltpu.HBM)


def sspec():
    return pl.BlockSpec(memory_space=pltpu.SMEM)


def dot_t(a, b):
    return lax.dot_general(a, b, (((1,), (1,)), ((), ())), preferred_element_type=F32)


def dot_n(a, b):
    return lax.dot_general(a, b, (((1,), (0,)), ((), ())), preferred_element_type=F32)


def call(body, out_shape, ins, specs, scratch=(), vmem=24, flops=0, nbytes=0, trans=0, outs=None):
    single = not isinstance(out_shape, (tuple, list))
    return pl.pallas_call(
        body,
        out_shape=out_shape,
        in_specs=specs,
        out_specs=vspec() if single else tuple(outs or [vspec() for _ in out_shape]),
        scratch_shapes=list(scratch),
        compiler_params=pltpu.CompilerParams(vmem_limit_bytes=vmem * 1024 * 1024),
        cost_estimate=pl.CostEstimate(flops=flops, bytes_accessed=nbytes, transcendentals=trans),
    )(*ins)


def head_id():
    return lax.axis_index("head") * lax.axis_size("req") + lax.axis_index("req")


def class_residue(c):
    j = head_id()
    r4 = lax.rem(j, 4)
    inner = lax.div(lax.rem(j, 16), 4)
    return 4 * lax.rem(c + inner, 4) + r4


def rank_in_block(own, first, k):
    grp = lax.shift_right_logical(own[first + k], 4)
    rank = jnp.int32(0)
    for e in range(k):
        rank += (lax.shift_right_logical(own[first + e], 4) == grp).astype(jnp.int32)
    return grp, rank


def start_kernel(
    own_h, dec, qkv, sent, q4, kvm_h, far, kvm, raw, own, wide, sem, part_sem, own_sem
):
    own_copy = pltpu.make_async_copy(own_h, own, own_sem)
    own_copy.start()
    me = lax.axis_index("req")
    rows = qkv.shape[1]
    parts = []
    for part in range(3):
        cp = pltpu.make_async_copy(qkv.at[part], raw.at[part], part_sem.at[part])
        cp.start()
        parts.append(cp)
    copies = []
    own_copy.wait()
    for b in range(8):
        src = [jnp.int32(0), jnp.int32(0)]
        for k in range(4):
            slot = own[4 * b + k]
            grp, rank = rank_in_block(own, 4 * b, k)
            mine = grp == me
            for r in range(2):
                src[r] = jnp.where(mine & (rank == r), slot & 15, src[r])
        for r in range(2):
            cp = pltpu.make_async_copy(dec.at[src[r]], sent.at[2 * b + r], sem.at[2 * b + r])
            cp.start()
            copies.append(cp)
    for part in range(3):
        parts[part].wait()
        wide[...] = raw[part].astype(F32)
        for c in range(4):
            start = class_residue(c)
            got = wide[pl.ds(start, rows // 16, stride=16), :].astype(BF16)
            at = pl.ds(128 * c, 128)
            if part == 0:
                for copy in range(4):
                    q4[copy, at, :] = got
            else:
                lanes = pl.ds(HD * (part - 1), HD)
                kvm[at, lanes] = got
                if c == 0:
                    far[:, lanes] = got
    keep = pltpu.make_async_copy(kvm, kvm_h, own_sem)
    keep.start()
    for cp in copies:
        cp.wait()
    keep.wait()


def both(m, l):
    count = m.shape[0]
    lane = lax.broadcasted_iota(jnp.int32, (count, HD), 1)
    return jnp.where(lane == 0, m, l)


def softmax_once(pieces, twice=False):
    m = functools.reduce(jnp.maximum, [jnp.max(s, axis=1, keepdims=True) for s, _ in pieces])
    l = 0.0
    acc = 0.0
    for s, v in pieces:
        p = jnp.exp2((s - m) * EXP_SCALE)
        if twice:
            col = lax.broadcasted_iota(jnp.int32, (1, s.shape[1]), 1)
            p = jnp.concatenate([p[:128] * jnp.where(col < 128, 2.0, 1.0), p[128:]], axis=0)
        l = l + jnp.sum(p, axis=1, keepdims=True)
        acc = acc + dot_n(p.astype(BF16), v)
    return m, l, acc


def combine(terms):
    top = functools.reduce(jnp.maximum, [t[0] for t in terms])
    length = 0.0
    total = 0.0
    for m, l, acc in terms:
        w = jnp.exp2((m - top) * EXP_SCALE)
        length = length + l * w
        total = total + acc * w
    return top, length, total


def term(acc, ml, at):
    pair = ml[at, :]
    return pair[:, 0:1], pair[:, 1:2], acc[at, :]


def near_kernel(
    raw, q4, kvm_h, col1, cache_h, near_o, acc_o, ml_o, cache, pass_on,
    kvm, acc_s, ml_s, sem,
):
    rows = raw.shape[1]
    step = 256
    load = pltpu.make_async_copy(kvm_h, kvm, sem.at[0])
    load.start()
    fetch = pltpu.make_async_copy(cache_h, cache, sem.at[1])
    fetch.start()
    pass_on[pl.ds(128, 128), :] = col1[...]
    inner = lax.div(lax.rem(head_id(), 16), 4)

    def order(dims, dim):
        a = lax.broadcasted_iota(jnp.int32, dims, dim)
        return 4 * (a & 127) + ((lax.shift_right_logical(a, 7) + inner) & 3)

    tri = lax.broadcasted_iota(jnp.int32, (step, step), 1) <= lax.broadcasted_iota(
        jnp.int32, (step, step), 0
    )
    for b in range(rows // step):
        at = pl.ds(step * b, step)
        q = raw[0, at, :]
        parts = [(jnp.where(tri, dot_t(q, raw[1, at, :]), NEG), raw[2, at, :])]
        if b:
            before = pl.ds(0, step * b)
            parts.append((dot_t(q, raw[1, before, :]), raw[2, before, :]))
        m, l, acc = softmax_once(parts)
        near_o[at, :] = (acc / l).astype(BF16)
        acc_s[at, :] = acc
        ml_s[at, :] = both(m, l)
    load.wait()
    pass_on[pl.ds(0, 128), :] = kvm[pl.ds(0, 128), :]
    s = dot_t(q4[0], kvm[:, pl.ds(0, HD)])
    s = jnp.where(order((1, 512), 1) <= order((512, 1), 0), s, NEG)
    m, l, acc = softmax_once([(s, kvm[:, pl.ds(HD, HD)])], True)
    acc_o[...] = acc
    ml_o[...] = both(m, l)
    for c in range(4):
        at = pl.ds(128 * c, 128)
        pick = pl.ds(class_residue(c), 128, stride=16)
        m, l, acc = combine([term(acc_s, ml_s, pick), term(acc_o, ml_o, at)])
        acc_o[at, :] = acc
        ml_o[at, :] = both(m, l)
    fetch.wait()


def pack(rows_m, rows_l):
    count = rows_m.shape[0]
    lane = lax.broadcasted_iota(jnp.int32, (count, HD), 1)
    st = jnp.zeros((count, HD), F32)
    for at, piece in enumerate(pieces(rows_m) + pieces(rows_l)):
        st = jnp.where(lane == at, piece, st)
    blocks = [st[128 * i : 128 * i + 128].T[:8] for i in range(count // 128)]
    if len(blocks) % 2:
        blocks.append(jnp.zeros((8, HD), F32))
    return jnp.concatenate(blocks, axis=0).astype(BF16)


def unpack(rows):
    st = rows.astype(F32)
    m = st[0:1] + st[1:2] + st[2:3]
    l = st[3:4] + st[4:5] + st[5:6]
    turned = jnp.concatenate([m, l, jnp.zeros((126, HD), F32)], axis=0).T
    return turned[:, 0:1], turned[:, 1:2]


def share_kernel(
    qs, kvm_h, col1, col2, acc_o, ml_o, back1, back2, back3,
    kvm, acc_1, ml_1, acc_2, ml_2, acc_3, ml_3, acc_f, ml_f, qf, kf, sem,
):
    load = pltpu.make_async_copy(kvm_h, kvm, sem)
    load.start()
    z = lax.axis_index("seq")
    local = lax.rem(z, 4)
    group = lax.div(z, 4)
    head = pl.ds(0, 128)
    tail = pl.ds(128, 384)
    keys, values = pl.ds(0, HD), pl.ds(HD, HD)

    def fill(valid, acc_r, ml_r, compute):
        @pl.when(valid)
        def _():
            m, l, acc = compute()
            acc_r[...] = acc
            ml_r[...] = both(m, l)

        @pl.when(jnp.logical_not(valid))
        def _():
            acc_r[...] = jnp.zeros((512, HD), F32)
            ml_r[...] = both(jnp.full((512, 1), NEG, F32), jnp.zeros((512, 1), F32))

    def far_level():
        for x in range(4):
            qf[pl.ds(128 * x, 128), :] = qs[local ^ x, head, :]
        kf[head, :] = col1[...]
        kf[pl.ds(128, 256), :] = col2[...]
        s = dot_t(qf[...], kf[:, keys])
        block = lax.shift_right_logical(lax.broadcasted_iota(jnp.int32, (1, 384), 1), 7)
        odd = (group & 1) == 1
        ok = jnp.where(block == 1, odd.astype(jnp.int32), (group >= 2).astype(jnp.int32))
        return softmax_once([(jnp.where(ok > 0, s, NEG), kf[:, values])])

    parts = ((1, acc_1, ml_1, back1), (2, acc_2, ml_2, back2), (3, acc_3, ml_3, back3))
    fill(group > 0, acc_f, ml_f, far_level)
    load.wait()
    for x, acc_r, ml_r, _ in parts:
        fill(
            (local ^ x) > local,
            acc_r,
            ml_r,
            lambda x=x: softmax_once(
                [(dot_t(qs[local ^ x], kvm[:, keys]), kvm[:, values])], True
            ),
        )

    def give(out, terms, rows):
        m, l, acc = combine(terms)
        out[rows, :] = (acc / jnp.where(l > 0.0, l, 1.0)).astype(BF16)
        return m, l

    for x, acc_r, ml_r, back in parts:
        far = term(acc_f, ml_f, pl.ds(128 * x, 128))
        m_a, l_a = give(back, [term(acc_r, ml_r, head), far], head)
        m_b, l_b = give(back, [term(acc_r, ml_r, tail)], tail)
        back[pl.ds(512, 32), :] = pack(
            jnp.concatenate([m_a, m_b], axis=0), jnp.concatenate([l_a, l_b], axis=0)
        )
    acc_o[...] = acc_f[head, :]
    ml_o[...] = ml_f[head, :]


def merge_kernel(near, acc, ml, acc_f, ml_f, back1, back2, back3, out, wide):
    wide[...] = near[...].astype(F32)
    for c in range(4):
        at = pl.ds(128 * c, 128)
        terms = [term(acc, ml, at)]
        if c == 0:
            terms.append(term(acc_f, ml_f, at))
        for part in (back1, back2, back3):
            stat = part[pl.ds(512 + 16 * (c // 2), 16), :][8 * (c % 2) : 8 * (c % 2) + 8]
            m, l = unpack(stat)
            terms.append((m, l, part[at, :].astype(F32) * l))
        _, length, total = combine(terms)
        wide[pl.ds(class_residue(c), 128, stride=16), :] = total / length
    out[...] = wide[...].astype(BF16)


def pieces(x):
    hi = x.astype(BF16).astype(F32)
    rest = x - hi
    mid = rest.astype(BF16).astype(F32)
    return hi, mid, (rest - mid).astype(BF16).astype(F32)


def cache_kernel(own, lens, arr, cache, out, o_s, st_s):
    z = lax.axis_index("seq")
    me = lax.axis_index("req")
    per = cache.shape[2]
    width = cache.shape[3]
    diag = lax.shift_right_logical(
        lax.broadcasted_iota(jnp.int32, (16, width), 1), 7
    ) == lax.shift_right_logical(lax.broadcasted_iota(jnp.int32, (16, width), 0), 1)
    token = lax.broadcasted_iota(jnp.int32, (16, 16), 0) & 1
    new_col = lax.broadcasted_iota(jnp.int32, (16, 16), 1)
    new_ok = (new_col <= token) & (z == 0)
    col = z * per + lax.broadcasted_iota(jnp.int32, (16, per), 1)
    row_head = lax.shift_right_logical(lax.broadcasted_iota(jnp.int32, (16, HD), 0), 1)
    lane = lax.broadcasted_iota(jnp.int32, (16, HD), 1)
    pad = jnp.zeros((14, width), F32)
    for k in range(4):
        grp, rank = rank_in_block(own, 4 * me, k)
        row = 2 * grp + rank
        q = arr[row, 0].astype(F32)
        qd = jnp.where(diag, jnp.concatenate([q] * 8, axis=0), 0.0).astype(BF16)
        kn = jnp.concatenate([arr[row, 1].astype(F32), pad], axis=0).astype(BF16)
        vn = jnp.concatenate([arr[row, 2].astype(F32), pad], axis=0).astype(BF16)
        c_ok = col < lens[4 * me + k]
        s_c = jnp.where(c_ok, dot_t(qd, cache[k, 0]), NEG)
        s_n = jnp.where(new_ok, dot_t(qd, kn), NEG)
        m = jnp.maximum(
            jnp.max(s_c, axis=1, keepdims=True), jnp.max(s_n, axis=1, keepdims=True)
        )
        p_c = jnp.where(c_ok, jnp.exp2((s_c - m) * EXP_SCALE), 0.0)
        p_n = jnp.where(new_ok, jnp.exp2((s_n - m) * EXP_SCALE), 0.0)
        l = jnp.sum(p_c, axis=1, keepdims=True) + jnp.sum(p_n, axis=1, keepdims=True)
        full = dot_n(p_c.astype(BF16), cache[k, 1]) + dot_n(p_n.astype(BF16), vn)
        o = jnp.zeros((16, HD), F32)
        for h in range(8):
            o = jnp.where(row_head == h, full[:, HD * h : HD * (h + 1)], o)
        o = o / jnp.where(l > 0.0, l, 1.0)
        st = jnp.zeros((16, HD), F32)
        for at, piece in enumerate(pieces(m) + pieces(l)):
            st = jnp.where(lane == at, piece, st)
        for h in range(8):
            o_s[pl.ds(8 * h + 2 * k, 2), :] = o[2 * h : 2 * h + 2]
            st_s[pl.ds(8 * h + 2 * k, 2), :] = st[2 * h : 2 * h + 2]
    values = o_s[...].astype(BF16)
    turned = st_s[...].T
    stats = jnp.concatenate([turned[:8, :], jnp.zeros((8, 64), F32)], axis=1).astype(BF16)
    for t in range(out.shape[0]):
        out[t, pl.ds(0, 64), :] = values
        out[t, pl.ds(64, 8), :] = stats


def project_kernel(own, got, weight, out):
    me = lax.axis_index("req")
    count = got.shape[0]
    ms, ls = [], []
    for t in range(count):
        st = got[t, pl.ds(64, 8), :].astype(F32)
        ms.append(st[0:1] + st[1:2] + st[2:3])
        ls.append(st[3:4] + st[4:5] + st[5:6])
    m = jnp.concatenate(ms, axis=0)
    l = jnp.concatenate(ls, axis=0)
    share = jnp.exp2((m - jnp.max(m, axis=0, keepdims=True)) * EXP_SCALE) * l
    share = share / jnp.sum(share, axis=0, keepdims=True)
    share = jnp.concatenate([share, jnp.zeros((128 - count, HD), F32)], axis=0).T
    total = jnp.zeros((64, HD), F32)
    for t in range(count):
        total = total + share[:64, t : t + 1] * got[t, pl.ds(0, 64), :].astype(F32)
    rows = jnp.concatenate([total[8 * h : 8 * h + 8] for h in range(8)], axis=1)
    y = dot_n(rows.astype(BF16), weight[...])
    out[...] = jnp.zeros(out.shape, BF16)
    seats = [rank_in_block(own, 4 * me, k) for k in range(4)]
    for h in range(4):
        cols = slice(64 * h, 64 * h + 64)
        lines = [
            jnp.concatenate([y[2 * k : 2 * k + 1, cols], y[2 * k + 1 : 2 * k + 2, cols]], axis=1)
            for k in range(4)
        ]
        for grp, _ in seats:
            pair = [jnp.zeros((1, HD), F32)] * 2
            for (other, rank), line in zip(seats, lines):
                for r in range(2):
                    pair[r] = jnp.where((other == grp) & (rank == r), line, pair[r])
            out[8 * h + grp] = jnp.concatenate(pair, axis=0).astype(BF16)


def settle_kernel(own, got, out):
    me = lax.axis_index("req")
    total = got[pl.ds(0, 8)].astype(F32)
    for h in range(1, 4):
        total = total + got[pl.ds(8 * h, 8)].astype(F32)
    out[...] = jnp.zeros(out.shape, BF16)
    for b in range(8):
        first = total[b]
        for k in range(4):
            slot = own[4 * b + k]
            grp, rank = rank_in_block(own, 4 * b, k)

            @pl.when(grp == me)
            def _(first=first, slot=slot, rank=rank):
                row = jnp.where(rank == 0, first[0:1], first[1:2])
                out[slot & 15] = jnp.concatenate([row[:, :64], row[:, 64:]], axis=0).astype(BF16)


def shape(dims, dtype=BF16):
    return jax.ShapeDtypeStruct(dims, dtype)


def staged(pre_qkv, cache_kv, dec_new, out_weight, owner_slot, prompt_lengths):
    qkv = jnp.swapaxes(pre_qkv, 0, 1)
    sent, q4, kvm, far = call(
        start_kernel,
        (
            shape(dec_new.shape),
            shape((4, 512, HD)),
            pltpu.HBM((512, 2 * HD), BF16),
            shape((128, 2 * HD)),
        ),
        (far_memory(owner_slot), far_memory(dec_new), far_memory(qkv)),
        [hspec(), hspec(), hspec()],
        [
            VMEM((512, 2 * HD), BF16),
            VMEM((3, 2048, HD), BF16),
            SMEM((32,), jnp.int32),
            VMEM((2048, HD), F32),
            pltpu.SemaphoreType.DMA((16,)),
            pltpu.SemaphoreType.DMA((3,)),
            pltpu.SemaphoreType.DMA,
        ],
        nbytes=4000000,
        outs=[vspec(), vspec(), hspec(), vspec()],
    )
    arrived = lax.all_to_all(sent, "req", 0, 0, tiled=True)
    rows4 = range(4)
    col1 = lax.ppermute(far, "seq", [(i, i + 12) for i in rows4] + [(i + 4, i + 8) for i in rows4])
    groups = [[4 * g + i for i in rows4] for g in rows4]
    qs = lax.all_to_all(q4, "seq", 0, 0, axis_index_groups=groups, tiled=True)

    def swap(x, bits):
        return lax.ppermute(x, "seq", [(i, i ^ bits) for i in range(16)])

    state = [shape((512, HD), F32)] * 2
    near_o, acc, ml, cache, pass_on = call(
        near_kernel,
        (shape((2048, HD)), *state, shape(cache_kv.shape), shape((256, 2 * HD))),
        (qkv, q4, far_memory(kvm), col1, far_memory(cache_kv)),
        [vspec(), vspec(), hspec(), vspec(), hspec()],
        [
            VMEM((512, 2 * HD), BF16),
            VMEM((2048, HD), F32),
            VMEM((2048, HD), F32),
            pltpu.SemaphoreType.DMA((2,)),
        ],
        flops=2 * 10**9,
        nbytes=3000000,
        trans=2 * 10**6,
    )
    col2 = lax.ppermute(
        pass_on,
        "seq",
        [(i + 8, i + 12) for i in rows4]
        + [(i + 12, i + 8) for i in rows4]
        + [(i, i + 4) for i in rows4],
    )
    partial = call(
        cache_kernel,
        shape((16, 72, HD)),
        (owner_slot, prompt_lengths, arrived, cache),
        [sspec(), sspec(), vspec(), vspec()],
        [VMEM((64, HD), F32), VMEM((64, HD), F32)],
        flops=10**8,
        nbytes=2000000,
    )
    parts = lax.all_to_all(partial, "seq", 0, 0, tiled=True)
    acc_f, ml_f, back1, back2, back3 = call(
        share_kernel,
        (*[shape((128, HD), F32)] * 2, *[shape((544, HD))] * 3),
        (qs, far_memory(kvm), col1, col2),
        [vspec(), hspec(), vspec(), vspec()],
        [VMEM((512, 2 * HD), BF16)]
        + [VMEM((512, HD), F32)] * 8
        + [VMEM((512, HD), BF16), VMEM((384, 2 * HD), BF16), pltpu.SemaphoreType.DMA],
        flops=10**9,
        nbytes=4000000,
        trans=10**6,
    )
    back1 = swap(back1, 1)
    back3 = swap(back3, 3)
    back2 = swap(back2, 2)
    answers = call(
        project_kernel,
        shape((32, 2, HD)),
        (owner_slot, parts, out_weight),
        [sspec(), vspec(), vspec()],
        flops=10**7,
        nbytes=1000000,
    )
    results = lax.all_to_all(answers, ("head", "req"), 0, 0, tiled=True)
    prefill_out = call(
        merge_kernel,
        shape((2048, HD)),
        (near_o, acc, ml, acc_f, ml_f, back1, back2, back3),
        [vspec()] * 8,
        [VMEM((2048, HD), F32)],
        flops=10**8,
        nbytes=4000000,
    )
    decode_out = call(
        settle_kernel,
        shape((16, 2, 64)),
        (owner_slot, results),
        [sspec(), vspec()],
        nbytes=100000,
    )
    return prefill_out, decode_out


def solution(mesh):
    return jax.shard_map(
        staged,
        mesh=mesh,
        in_specs=(
            P("seq", None, ("head", "req")),
            P("req", None, "seq", "head"),
            P("req", None, None, "head"),
            P("head", "seq"),
            P(),
            P(),
        ),
        out_specs=(P("seq", ("head", "req")), P("req", None, ("seq", "head"))),
        check_vma=False,
    )
```

```python
import functools
import math

import jax
import jax.numpy as jnp
from jax import lax
from jax.experimental import pallas as pl
from jax.experimental.pallas import tpu as pltpu
from jax.sharding import PartitionSpec as P

HD = 128
NEG = -1e30
EXP_SCALE = HD**-0.5 * math.log2(math.e)
F32 = jnp.float32
BF16 = jnp.bfloat16

VMEM = pltpu.VMEM
SMEM = pltpu.SMEM


def vspec():
    return pl.BlockSpec(memory_space=pltpu.VMEM)


def far_memory(x):
    return pltpu.with_memory_space_constraint(x, pltpu.HBM)


def hspec():
    return pl.BlockSpec(memory_space=pltpu.HBM)


def sspec():
    return pl.BlockSpec(memory_space=pltpu.SMEM)


def dot_t(a, b):
    return lax.dot_general(a, b, (((1,), (1,)), ((), ())), preferred_element_type=F32)


def dot_n(a, b):
    return lax.dot_general(a, b, (((1,), (0,)), ((), ())), preferred_element_type=F32)


def call(body, out_shape, ins, specs, scratch=(), vmem=24, flops=0, nbytes=0, trans=0, outs=None):
    single = not isinstance(out_shape, (tuple, list))
    return pl.pallas_call(
        body,
        out_shape=out_shape,
        in_specs=specs,
        out_specs=vspec() if single else tuple(outs or [vspec() for _ in out_shape]),
        scratch_shapes=list(scratch),
        compiler_params=pltpu.CompilerParams(vmem_limit_bytes=vmem * 1024 * 1024),
        cost_estimate=pl.CostEstimate(flops=flops, bytes_accessed=nbytes, transcendentals=trans),
    )(*ins)


def head_id():
    return lax.axis_index("head") * lax.axis_size("req") + lax.axis_index("req")


def class_residue(c):
    j = head_id()
    r4 = lax.rem(j, 4)
    inner = lax.div(lax.rem(j, 16), 4)
    return 4 * lax.rem(c + inner, 4) + r4


def rank_in_block(own, first, k):
    grp = lax.shift_right_logical(own[first + k], 4)
    rank = jnp.int32(0)
    for e in range(k):
        rank += (lax.shift_right_logical(own[first + e], 4) == grp).astype(jnp.int32)
    return grp, rank


def start_kernel(
    own_h, dec, qkv, raw, sent, qm, ask, msg, far, own, wide, sem, part_sem, own_sem
):
    own_copy = pltpu.make_async_copy(own_h, own, own_sem)
    own_copy.start()
    me = lax.axis_index("req")
    rows = qkv.shape[1]
    parts = []
    for part in range(3):
        cp = pltpu.make_async_copy(qkv.at[part], raw.at[part], part_sem.at[part])
        cp.start()
        parts.append(cp)
    copies = []
    own_copy.wait()
    for b in range(8):
        src = [jnp.int32(0), jnp.int32(0)]
        for k in range(4):
            slot = own[4 * b + k]
            grp, rank = rank_in_block(own, 4 * b, k)
            mine = grp == me
            for r in range(2):
                src[r] = jnp.where(mine & (rank == r), slot & 15, src[r])
        for r in range(2):
            cp = pltpu.make_async_copy(dec.at[src[r]], sent.at[2 * b + r], sem.at[2 * b + r])
            cp.start()
            copies.append(cp)
    for part in range(3):
        parts[part].wait()
        wide[...] = raw[part].astype(F32)
        for c in range(4):
            start = class_residue(c)
            got = wide[pl.ds(start, rows // 16, stride=16), :].astype(BF16)
            at = pl.ds(128 * c, 128)
            if part == 0:
                qm[at, :] = got
                if c == 0:
                    ask[...] = got
                    msg[pl.ds(512, 64), pl.ds(0, HD)] = got[:64]
                    msg[pl.ds(512, 64), pl.ds(HD, HD)] = got[64:]
            else:
                lanes = pl.ds(HD * (part - 1), HD)
                msg[at, lanes] = got
                if c == 0:
                    far[:, lanes] = got
    for cp in copies:
        cp.wait()


def both(m, l):
    count = m.shape[0]
    lane = lax.broadcasted_iota(jnp.int32, (count, HD), 1)
    return jnp.where(lane == 0, m, l)


def softmax_once(pieces, twice=False):
    m = functools.reduce(jnp.maximum, [jnp.max(s, axis=1, keepdims=True) for s, _ in pieces])
    l = 0.0
    acc = 0.0
    for s, v in pieces:
        p = jnp.exp2((s - m) * EXP_SCALE)
        if twice:
            col = lax.broadcasted_iota(jnp.int32, (1, s.shape[1]), 1)
            p = jnp.concatenate([p[:128] * jnp.where(col < 128, 2.0, 1.0), p[128:]], axis=0)
        l = l + jnp.sum(p, axis=1, keepdims=True)
        acc = acc + dot_n(p.astype(BF16), v)
    return m, l, acc


def combine(terms):
    top = functools.reduce(jnp.maximum, [t[0] for t in terms])
    length = 0.0
    total = 0.0
    for m, l, acc in terms:
        w = jnp.exp2((m - top) * EXP_SCALE)
        length = length + l * w
        total = total + acc * w
    return top, length, total


def term(acc, ml, at):
    pair = ml[at, :]
    return pair[:, 0:1], pair[:, 1:2], acc[at, :]


def near_kernel(
    raw, qm, msg, near_h, acc_h, ml_h,
    acc_s, ml_s, near_o, acc_o, ml_o, sem, out_sem,
):
    rows = raw.shape[1]
    step = 256
    copies = []
    inner = lax.div(lax.rem(head_id(), 16), 4)

    def order(dims, dim):
        a = lax.broadcasted_iota(jnp.int32, dims, dim)
        return 4 * (a & 127) + ((lax.shift_right_logical(a, 7) + inner) & 3)

    mine = pl.ds(0, 512)
    s = dot_t(qm[...], msg[mine, pl.ds(0, HD)])
    s = jnp.where(order((1, 512), 1) <= order((512, 1), 0), s, NEG)
    m, l, acc = softmax_once([(s, msg[mine, pl.ds(HD, HD)])], True)
    acc_o[...] = acc
    ml_o[...] = both(m, l)
    tri = lax.broadcasted_iota(jnp.int32, (step, step), 1) <= lax.broadcasted_iota(
        jnp.int32, (step, step), 0
    )
    for b in range(rows // step):
        at = pl.ds(step * b, step)
        q = raw[0, at, :]
        parts = [(jnp.where(tri, dot_t(q, raw[1, at, :]), NEG), raw[2, at, :])]
        if b:
            before = pl.ds(0, step * b)
            parts.append((dot_t(q, raw[1, before, :]), raw[2, before, :]))
        m, l, acc = softmax_once(parts)
        near_o[at, :] = (acc / l).astype(BF16)
        cp = pltpu.make_async_copy(near_o.at[at], near_h.at[at], out_sem.at[b])
        cp.start()
        copies.append(cp)
        acc_s[at, :] = acc
        ml_s[at, :] = both(m, l)
    for c in range(4):
        at = pl.ds(128 * c, 128)
        pick = pl.ds(class_residue(c), 128, stride=16)
        m, l, acc = combine([term(acc_s, ml_s, pick), term(acc_o, ml_o, at)])
        acc_o[at, :] = acc
        ml_o[at, :] = both(m, l)
    for i, (src, dst) in enumerate(((acc_o, acc_h), (ml_o, ml_h))):
        cp = pltpu.make_async_copy(src, dst, sem.at[i])
        cp.start()
        copies.append(cp)
    for cp in copies:
        cp.wait()


def pack(rows_m, rows_l):
    count = rows_m.shape[0]
    lane = lax.broadcasted_iota(jnp.int32, (count, HD), 1)
    st = jnp.zeros((count, HD), F32)
    for at, piece in enumerate(pieces(rows_m) + pieces(rows_l)):
        st = jnp.where(lane == at, piece, st)
    blocks = [st[128 * i : 128 * i + 128].T[:8] for i in range(count // 128)]
    if len(blocks) % 2:
        blocks.append(jnp.zeros((8, HD), F32))
    return jnp.concatenate(blocks, axis=0).astype(BF16)


def unpack(rows):
    st = rows.astype(F32)
    m = st[0:1] + st[1:2] + st[2:3]
    l = st[3:4] + st[4:5] + st[5:6]
    turned = jnp.concatenate([m, l, jnp.zeros((126, HD), F32)], axis=0).T
    return turned[:, 0:1], turned[:, 1:2]


def share_kernel(
    qm, msg, got1, got2, got3, col1, col2, col3, acc_h, ml_h,
    acc_o, ml_o, back1, back2, back3,
    acc_n, ml_n, acc_m, ml_m, acc_2, ml_2, acc_f, ml_f, qf, kf, sem,
):
    z = lax.axis_index("seq")
    local = lax.rem(z, 4)
    group = lax.div(z, 4)
    load_acc = pltpu.make_async_copy(acc_h, acc_n, sem.at[0])
    load_ml = pltpu.make_async_copy(ml_h, ml_n, sem.at[1])
    load_acc.start()
    load_ml.start()
    one = pl.ds(0, 512)
    head = pl.ds(0, 128)
    tail = pl.ds(128, 384)
    keys, values = pl.ds(0, HD), pl.ds(HD, HD)

    def fill(valid, acc_r, ml_r, compute):
        @pl.when(valid)
        def _():
            m, l, acc = compute()
            acc_r[...] = acc
            ml_r[...] = both(m, l)

        @pl.when(jnp.logical_not(valid))
        def _():
            acc_r[...] = jnp.zeros((512, HD), F32)
            ml_r[...] = both(jnp.full((512, 1), NEG, F32), jnp.zeros((512, 1), F32))

    def other_pair():
        q = got2[...]
        return softmax_once(
            [
                (dot_t(q, msg[one, keys]), msg[one, values]),
                (dot_t(q, got1[one, keys]), got1[one, values]),
            ],
            True,
        )

    def own_pair():
        return softmax_once([(dot_t(qm[...], got1[one, keys]), got1[one, values])], True)

    def far_level():
        half = pl.ds(512, 64)
        qf[pl.ds(0, 128), :] = qm[head, :]
        qf[pl.ds(128, 128), :] = got2[head, :]
        qf[pl.ds(256, 64), :] = got1[half, keys]
        qf[pl.ds(320, 64), :] = got1[half, values]
        qf[pl.ds(384, 128), :] = got3[...]
        for i, col in enumerate((col1, col2, col3)):
            kf[pl.ds(128 * i, 128), :] = col[...]
        s = dot_t(qf[...], kf[:, keys])
        at = lax.broadcasted_iota(jnp.int32, (1, 384), 1)
        return softmax_once([(jnp.where(at < 128 * group, s, NEG), kf[:, values])])

    fill(local < 2, acc_2, ml_2, other_pair)
    fill((local & 1) == 1, acc_m, ml_m, own_pair)
    fill(group > 0, acc_f, ml_f, far_level)

    def give(out, terms, rows):
        m, l, acc = combine(terms)
        out[rows, :] = (acc / jnp.where(l > 0.0, l, 1.0)).astype(BF16)
        return m, l

    far2 = term(acc_f, ml_f, pl.ds(128, 128))
    m_a, l_a = give(back2, [term(acc_2, ml_2, head), far2], head)
    m_b, l_b = give(back2, [term(acc_2, ml_2, tail)], tail)
    back2[pl.ds(512, 32), :] = pack(
        jnp.concatenate([m_a, m_b], axis=0), jnp.concatenate([l_a, l_b], axis=0)
    )
    for out, first in ((back1, 256), (back3, 384)):
        m, l = give(out, [term(acc_f, ml_f, pl.ds(first, 128))], head)
        out[pl.ds(128, 16), :] = pack(m, l)
    load_acc.wait()
    load_ml.wait()
    for at in (head, tail):
        terms = [term(acc_n, ml_n, at), term(acc_m, ml_m, at)]
        if at is head:
            terms.append(term(acc_f, ml_f, head))
        m, l, acc = combine(terms)
        acc_n[at, :] = acc
        ml_n[at, :] = both(m, l)
    save_acc = pltpu.make_async_copy(acc_n, acc_o, sem.at[0])
    save_ml = pltpu.make_async_copy(ml_n, ml_o, sem.at[1])
    save_acc.start()
    save_ml.start()
    save_acc.wait()
    save_ml.wait()


def merge_kernel(near_h, acc_h, ml_h, back1, back2, back3, out, near, acc, ml, wide, sem):
    copies = [
        pltpu.make_async_copy(src, dst, sem.at[i])
        for i, (src, dst) in enumerate(((near_h, near), (acc_h, acc), (ml_h, ml)))
    ]
    for cp in copies:
        cp.start()
    for cp in copies:
        cp.wait()
    wide[...] = near[...].astype(F32)
    for c in range(4):
        at = pl.ds(128 * c, 128)
        terms = [(ml[at, :][:, 0:1], ml[at, :][:, 1:2], acc[at, :])]
        for part, rows, stat in ((back2, 128 * c, 512 + 8 * c), (back1, 0, 128), (back3, 0, 128)):
            if c and part is not back2:
                continue
            pm, plen = unpack(part[pl.ds(stat // 16 * 16, 16), :][stat % 16 : stat % 16 + 8])
            terms.append((pm, plen, part[pl.ds(rows, 128), :].astype(F32) * plen))
        top = functools.reduce(jnp.maximum, [t[0] for t in terms])
        total = 0.0
        length = 0.0
        for tm, tl, ta in terms:
            w = jnp.exp2((tm - top) * EXP_SCALE)
            length = length + tl * w
            total = total + ta * w
        wide[pl.ds(class_residue(c), 128, stride=16), :] = total / length
    out[...] = wide[...].astype(BF16)


def pieces(x):
    hi = x.astype(BF16).astype(F32)
    rest = x - hi
    mid = rest.astype(BF16).astype(F32)
    return hi, mid, (rest - mid).astype(BF16).astype(F32)


def cache_kernel(own, lens, arr, cache, out, o_s, st_s):
    z = lax.axis_index("seq")
    me = lax.axis_index("req")
    per = cache.shape[2]
    width = cache.shape[3]
    diag = lax.shift_right_logical(
        lax.broadcasted_iota(jnp.int32, (16, width), 1), 7
    ) == lax.shift_right_logical(lax.broadcasted_iota(jnp.int32, (16, width), 0), 1)
    token = lax.broadcasted_iota(jnp.int32, (16, 16), 0) & 1
    new_col = lax.broadcasted_iota(jnp.int32, (16, 16), 1)
    new_ok = (new_col <= token) & (z == 0)
    col = z * per + lax.broadcasted_iota(jnp.int32, (16, per), 1)
    row_head = lax.shift_right_logical(lax.broadcasted_iota(jnp.int32, (16, HD), 0), 1)
    lane = lax.broadcasted_iota(jnp.int32, (16, HD), 1)
    pad = jnp.zeros((14, width), F32)
    for k in range(4):
        grp, rank = rank_in_block(own, 4 * me, k)
        row = 2 * grp + rank
        q = arr[row, 0].astype(F32)
        qd = jnp.where(diag, jnp.concatenate([q] * 8, axis=0), 0.0).astype(BF16)
        kn = jnp.concatenate([arr[row, 1].astype(F32), pad], axis=0).astype(BF16)
        vn = jnp.concatenate([arr[row, 2].astype(F32), pad], axis=0).astype(BF16)
        c_ok = col < lens[4 * me + k]
        s_c = jnp.where(c_ok, dot_t(qd, cache[k, 0]), NEG)
        s_n = jnp.where(new_ok, dot_t(qd, kn), NEG)
        m = jnp.maximum(
            jnp.max(s_c, axis=1, keepdims=True), jnp.max(s_n, axis=1, keepdims=True)
        )
        p_c = jnp.where(c_ok, jnp.exp2((s_c - m) * EXP_SCALE), 0.0)
        p_n = jnp.where(new_ok, jnp.exp2((s_n - m) * EXP_SCALE), 0.0)
        l = jnp.sum(p_c, axis=1, keepdims=True) + jnp.sum(p_n, axis=1, keepdims=True)
        full = dot_n(p_c.astype(BF16), cache[k, 1]) + dot_n(p_n.astype(BF16), vn)
        o = jnp.zeros((16, HD), F32)
        for h in range(8):
            o = jnp.where(row_head == h, full[:, HD * h : HD * (h + 1)], o)
        o = o / jnp.where(l > 0.0, l, 1.0)
        st = jnp.zeros((16, HD), F32)
        for at, piece in enumerate(pieces(m) + pieces(l)):
            st = jnp.where(lane == at, piece, st)
        for h in range(8):
            o_s[pl.ds(8 * h + 2 * k, 2), :] = o[2 * h : 2 * h + 2]
            st_s[pl.ds(8 * h + 2 * k, 2), :] = st[2 * h : 2 * h + 2]
    values = o_s[...].astype(BF16)
    turned = st_s[...].T
    stats = jnp.concatenate([turned[:8, :], jnp.zeros((8, 64), F32)], axis=1).astype(BF16)
    for t in range(out.shape[0]):
        out[t, pl.ds(0, 64), :] = values
        out[t, pl.ds(64, 8), :] = stats


def project_kernel(own, got, weight, out):
    me = lax.axis_index("req")
    count = got.shape[0]
    ms, ls = [], []
    for t in range(count):
        st = got[t, pl.ds(64, 8), :].astype(F32)
        ms.append(st[0:1] + st[1:2] + st[2:3])
        ls.append(st[3:4] + st[4:5] + st[5:6])
    m = jnp.concatenate(ms, axis=0)
    l = jnp.concatenate(ls, axis=0)
    share = jnp.exp2((m - jnp.max(m, axis=0, keepdims=True)) * EXP_SCALE) * l
    share = share / jnp.sum(share, axis=0, keepdims=True)
    share = jnp.concatenate([share, jnp.zeros((128 - count, HD), F32)], axis=0).T
    total = jnp.zeros((64, HD), F32)
    for t in range(count):
        total = total + share[:64, t : t + 1] * got[t, pl.ds(0, 64), :].astype(F32)
    rows = jnp.concatenate([total[8 * h : 8 * h + 8] for h in range(8)], axis=1)
    y = dot_n(rows.astype(BF16), weight[...])
    out[...] = jnp.zeros(out.shape, BF16)
    seats = [rank_in_block(own, 4 * me, k) for k in range(4)]
    for h in range(4):
        cols = slice(64 * h, 64 * h + 64)
        lines = [
            jnp.concatenate([y[2 * k : 2 * k + 1, cols], y[2 * k + 1 : 2 * k + 2, cols]], axis=1)
            for k in range(4)
        ]
        for grp, _ in seats:
            pair = [jnp.zeros((1, HD), F32)] * 2
            for (other, rank), line in zip(seats, lines):
                for r in range(2):
                    pair[r] = jnp.where((other == grp) & (rank == r), line, pair[r])
            out[8 * h + grp] = jnp.concatenate(pair, axis=0).astype(BF16)


def settle_kernel(own, got, out):
    me = lax.axis_index("req")
    total = got[pl.ds(0, 8)].astype(F32)
    for h in range(1, 4):
        total = total + got[pl.ds(8 * h, 8)].astype(F32)
    out[...] = jnp.zeros(out.shape, BF16)
    for b in range(8):
        first = total[b]
        for k in range(4):
            slot = own[4 * b + k]
            grp, rank = rank_in_block(own, 4 * b, k)

            @pl.when(grp == me)
            def _(first=first, slot=slot, rank=rank):
                row = jnp.where(rank == 0, first[0:1], first[1:2])
                out[slot & 15] = jnp.concatenate([row[:, :64], row[:, 64:]], axis=0).astype(BF16)


def shape(dims, dtype=BF16):
    return jax.ShapeDtypeStruct(dims, dtype)


def staged(pre_qkv, cache_kv, dec_new, out_weight, owner_slot, prompt_lengths):
    qkv = jnp.swapaxes(pre_qkv, 0, 1)
    raw, sent, qm, ask, msg, far = call(
        start_kernel,
        (
            shape((3, 2048, HD)),
            shape(dec_new.shape),
            shape((512, HD)),
            shape((128, HD)),
            shape((576, 2 * HD)),
            shape((128, 2 * HD)),
        ),
        (far_memory(owner_slot), far_memory(dec_new), far_memory(qkv)),
        [hspec(), hspec(), hspec()],
        [
            SMEM((32,), jnp.int32),
            VMEM((2048, HD), F32),
            pltpu.SemaphoreType.DMA((16,)),
            pltpu.SemaphoreType.DMA((3,)),
            pltpu.SemaphoreType.DMA,
        ],
        nbytes=4000000,
    )
    arrived = lax.all_to_all(sent, "req", 0, 0, tiled=True)

    def swap(x, bits):
        return lax.ppermute(x, "seq", [(i, i ^ bits) for i in range(16)])

    def relay(x, first, stop, hop):
        return lax.ppermute(x, "seq", [(i, i + hop) for i in range(first, stop)])

    col1 = relay(far, 0, 12, 4)
    col3 = relay(far, 0, 4, 12)
    got3 = swap(ask, 3)
    got2 = swap(qm, 2)
    got1 = swap(msg, 1)
    col2 = relay(col1, 4, 12, 4)
    state = [pltpu.HBM((512, HD), F32)] * 2
    near_o, acc, ml = call(
        near_kernel,
        (pltpu.HBM((2048, HD), BF16), *state),
        (raw, qm, msg),
        [vspec()] * 3,
        [
            VMEM((2048, HD), F32),
            VMEM((2048, HD), F32),
            VMEM((2048, HD), BF16),
            VMEM((512, HD), F32),
            VMEM((512, HD), F32),
            pltpu.SemaphoreType.DMA((8,)),
            pltpu.SemaphoreType.DMA((8,)),
        ],
        flops=2 * 10**9,
        nbytes=3000000,
        trans=2 * 10**6,
        outs=[hspec()] * 3,
    )
    partial = call(
        cache_kernel,
        shape((16, 72, HD)),
        (owner_slot, prompt_lengths, arrived, cache_kv),
        [sspec(), sspec(), vspec(), vspec()],
        [VMEM((64, HD), F32), VMEM((64, HD), F32)],
        flops=10**8,
        nbytes=2000000,
    )
    parts = lax.all_to_all(partial, "seq", 0, 0, tiled=True)
    acc, ml, back1, back2, back3 = call(
        share_kernel,
        (*state, shape((144, HD)), shape((544, HD)), shape((144, HD))),
        (qm, msg, got1, got2, got3, col1, col2, col3, far_memory(acc), far_memory(ml)),
        [vspec()] * 8 + [hspec()] * 2,
        [VMEM((512, HD), F32)] * 8
        + [VMEM((512, HD), BF16), VMEM((384, 2 * HD), BF16), pltpu.SemaphoreType.DMA((2,))],
        flops=10**9,
        nbytes=4000000,
        trans=10**6,
        outs=[hspec()] * 2 + [vspec()] * 3,
    )
    back1 = swap(back1, 1)
    back3 = swap(back3, 3)
    back2 = swap(back2, 2)
    answers = call(
        project_kernel,
        shape((32, 2, HD)),
        (owner_slot, parts, out_weight),
        [sspec(), vspec(), vspec()],
        flops=10**7,
        nbytes=1000000,
    )
    results = lax.all_to_all(answers, ("head", "req"), 0, 0, tiled=True)
    prefill_out = call(
        merge_kernel,
        shape((2048, HD)),
        (far_memory(near_o), far_memory(acc), far_memory(ml), back1, back2, back3),
        [hspec()] * 3 + [vspec()] * 3,
        [
            VMEM((2048, HD), BF16),
            VMEM((512, HD), F32),
            VMEM((512, HD), F32),
            VMEM((2048, HD), F32),
            pltpu.SemaphoreType.DMA((3,)),
        ],
        flops=10**8,
        nbytes=4000000,
    )
    decode_out = call(
        settle_kernel,
        shape((16, 2, 64)),
        (owner_slot, results),
        [sspec(), vspec()],
        nbytes=100000,
    )
    return prefill_out, decode_out


def solution(mesh):
    return jax.shard_map(
        staged,
        mesh=mesh,
        in_specs=(
            P("seq", None, ("head", "req")),
            P("req", None, "seq", "head"),
            P("req", None, None, "head"),
            P("head", "seq"),
            P(),
            P(),
        ),
        out_specs=(P("seq", ("head", "req")), P("req", None, ("seq", "head"))),
        check_vma=False,
    )
```

```python
import functools
import math

import jax
import jax.numpy as jnp
from jax import lax
from jax.experimental import pallas as pl
from jax.experimental.pallas import tpu as pltpu
from jax.sharding import PartitionSpec as P

HD = 128
NEG = -1e30
EXP_SCALE = HD**-0.5 * math.log2(math.e)
F32 = jnp.float32
BF16 = jnp.bfloat16

VMEM = pltpu.VMEM
SMEM = pltpu.SMEM


def vspec():
    return pl.BlockSpec(memory_space=pltpu.VMEM)


def far_memory(x):
    return pltpu.with_memory_space_constraint(x, pltpu.HBM)


def hspec():
    return pl.BlockSpec(memory_space=pltpu.HBM)


def sspec():
    return pl.BlockSpec(memory_space=pltpu.SMEM)


def dot_t(a, b):
    return lax.dot_general(a, b, (((1,), (1,)), ((), ())), preferred_element_type=F32)


def dot_n(a, b):
    return lax.dot_general(a, b, (((1,), (0,)), ((), ())), preferred_element_type=F32)


def call(body, out_shape, ins, specs, scratch=(), vmem=24, flops=0, nbytes=0, trans=0, outs=None):
    single = not isinstance(out_shape, (tuple, list))
    return pl.pallas_call(
        body,
        out_shape=out_shape,
        in_specs=specs,
        out_specs=vspec() if single else tuple(outs or [vspec() for _ in out_shape]),
        scratch_shapes=list(scratch),
        compiler_params=pltpu.CompilerParams(vmem_limit_bytes=vmem * 1024 * 1024),
        cost_estimate=pl.CostEstimate(flops=flops, bytes_accessed=nbytes, transcendentals=trans),
    )(*ins)


def head_id():
    return lax.axis_index("head") * lax.axis_size("req") + lax.axis_index("req")


def class_residue(c):
    j = head_id()
    r4 = lax.rem(j, 4)
    inner = lax.div(lax.rem(j, 16), 4)
    return 4 * lax.rem(c + inner, 4) + r4


def rank_in_block(own, first, k):
    grp = lax.shift_right_logical(own[first + k], 4)
    rank = jnp.int32(0)
    for e in range(k):
        rank += (lax.shift_right_logical(own[first + e], 4) == grp).astype(jnp.int32)
    return grp, rank


def start_kernel(
    own_h, dec, qkv, raw, sent, qm, ask, msg, far, own, wide, sem, part_sem, own_sem
):
    own_copy = pltpu.make_async_copy(own_h, own, own_sem)
    own_copy.start()
    me = lax.axis_index("req")
    rows = qkv.shape[1]
    parts = []
    for part in range(3):
        cp = pltpu.make_async_copy(qkv.at[part], raw.at[part], part_sem.at[part])
        cp.start()
        parts.append(cp)
    copies = []
    own_copy.wait()
    for b in range(8):
        src = [jnp.int32(0), jnp.int32(0)]
        for k in range(4):
            slot = own[4 * b + k]
            grp, rank = rank_in_block(own, 4 * b, k)
            mine = grp == me
            for r in range(2):
                src[r] = jnp.where(mine & (rank == r), slot & 15, src[r])
        for r in range(2):
            cp = pltpu.make_async_copy(dec.at[src[r]], sent.at[2 * b + r], sem.at[2 * b + r])
            cp.start()
            copies.append(cp)
    for part in range(3):
        parts[part].wait()
        wide[...] = raw[part].astype(F32)
        for c in range(4):
            start = class_residue(c)
            got = wide[pl.ds(start, rows // 16, stride=16), :].astype(BF16)
            at = pl.ds(128 * c, 128)
            if part == 0:
                qm[at, :] = got
                if c == 0:
                    ask[...] = got
                    msg[pl.ds(512, 64), pl.ds(0, HD)] = got[:64]
                    msg[pl.ds(512, 64), pl.ds(HD, HD)] = got[64:]
            else:
                lanes = pl.ds(HD * (part - 1), HD)
                msg[at, lanes] = got
                if c == 0:
                    far[:, lanes] = got
    for cp in copies:
        cp.wait()


def both(m, l):
    count = m.shape[0]
    lane = lax.broadcasted_iota(jnp.int32, (count, HD), 1)
    return jnp.where(lane == 0, m, l)


def softmax_once(pieces, twice=False):
    m = functools.reduce(jnp.maximum, [jnp.max(s, axis=1, keepdims=True) for s, _ in pieces])
    l = 0.0
    acc = 0.0
    for s, v in pieces:
        p = jnp.exp2((s - m) * EXP_SCALE)
        if twice:
            col = lax.broadcasted_iota(jnp.int32, (1, s.shape[1]), 1)
            p = jnp.concatenate([p[:128] * jnp.where(col < 128, 2.0, 1.0), p[128:]], axis=0)
        l = l + jnp.sum(p, axis=1, keepdims=True)
        acc = acc + dot_n(p.astype(BF16), v)
    return m, l, acc


def combine(terms):
    top = functools.reduce(jnp.maximum, [t[0] for t in terms])
    length = 0.0
    total = 0.0
    for m, l, acc in terms:
        w = jnp.exp2((m - top) * EXP_SCALE)
        length = length + l * w
        total = total + acc * w
    return top, length, total


def term(acc, ml, at):
    pair = ml[at, :]
    return pair[:, 0:1], pair[:, 1:2], acc[at, :]


def near_kernel(
    raw, qm, msg, near_h, acc_h, ml_h,
    acc_s, ml_s, near_o, acc_o, ml_o, sem, out_sem,
):
    rows = raw.shape[1]
    step = 256
    copies = []
    inner = lax.div(lax.rem(head_id(), 16), 4)

    def order(dims, dim):
        a = lax.broadcasted_iota(jnp.int32, dims, dim)
        return 4 * (a & 127) + ((lax.shift_right_logical(a, 7) + inner) & 3)

    mine = pl.ds(0, 512)
    s = dot_t(qm[...], msg[mine, pl.ds(0, HD)])
    s = jnp.where(order((1, 512), 1) <= order((512, 1), 0), s, NEG)
    m, l, acc = softmax_once([(s, msg[mine, pl.ds(HD, HD)])], True)
    acc_o[...] = acc
    ml_o[...] = both(m, l)
    tri = lax.broadcasted_iota(jnp.int32, (step, step), 1) <= lax.broadcasted_iota(
        jnp.int32, (step, step), 0
    )
    for b in range(rows // step):
        at = pl.ds(step * b, step)
        q = raw[0, at, :]
        parts = [(jnp.where(tri, dot_t(q, raw[1, at, :]), NEG), raw[2, at, :])]
        if b:
            before = pl.ds(0, step * b)
            parts.append((dot_t(q, raw[1, before, :]), raw[2, before, :]))
        m, l, acc = softmax_once(parts)
        near_o[at, :] = (acc / l).astype(BF16)
        cp = pltpu.make_async_copy(near_o.at[at], near_h.at[at], out_sem.at[b])
        cp.start()
        copies.append(cp)
        acc_s[at, :] = acc
        ml_s[at, :] = both(m, l)
    for c in range(4):
        at = pl.ds(128 * c, 128)
        pick = pl.ds(class_residue(c), 128, stride=16)
        m, l, acc = combine([term(acc_s, ml_s, pick), term(acc_o, ml_o, at)])
        acc_o[at, :] = acc
        ml_o[at, :] = both(m, l)
    for i, (src, dst) in enumerate(((acc_o, acc_h), (ml_o, ml_h))):
        cp = pltpu.make_async_copy(src, dst, sem.at[i])
        cp.start()
        copies.append(cp)
    for cp in copies:
        cp.wait()


def pack(rows_m, rows_l):
    count = rows_m.shape[0]
    lane = lax.broadcasted_iota(jnp.int32, (count, HD), 1)
    st = jnp.zeros((count, HD), F32)
    for at, piece in enumerate(pieces(rows_m) + pieces(rows_l)):
        st = jnp.where(lane == at, piece, st)
    blocks = [st[128 * i : 128 * i + 128].T[:8] for i in range(count // 128)]
    if len(blocks) % 2:
        blocks.append(jnp.zeros((8, HD), F32))
    return jnp.concatenate(blocks, axis=0).astype(BF16)


def unpack(rows):
    st = rows.astype(F32)
    m = st[0:1] + st[1:2] + st[2:3]
    l = st[3:4] + st[4:5] + st[5:6]
    turned = jnp.concatenate([m, l, jnp.zeros((126, HD), F32)], axis=0).T
    return turned[:, 0:1], turned[:, 1:2]


def share_kernel(
    qm, msg, got1, got2, got3, col1, col2, col3, acc_h, ml_h,
    acc_o, ml_o, back1, back2, back3,
    acc_n, ml_n, acc_m, ml_m, acc_2, ml_2, acc_f, ml_f, qf, kf, sem,
):
    z = lax.axis_index("seq")
    local = lax.rem(z, 4)
    group = lax.div(z, 4)
    load_acc = pltpu.make_async_copy(acc_h, acc_n, sem.at[0])
    load_ml = pltpu.make_async_copy(ml_h, ml_n, sem.at[1])
    load_acc.start()
    load_ml.start()
    one = pl.ds(0, 512)
    head = pl.ds(0, 128)
    tail = pl.ds(128, 384)
    keys, values = pl.ds(0, HD), pl.ds(HD, HD)

    def fill(valid, acc_r, ml_r, compute):
        @pl.when(valid)
        def _():
            m, l, acc = compute()
            acc_r[...] = acc
            ml_r[...] = both(m, l)

        @pl.when(jnp.logical_not(valid))
        def _():
            acc_r[...] = jnp.zeros((512, HD), F32)
            ml_r[...] = both(jnp.full((512, 1), NEG, F32), jnp.zeros((512, 1), F32))

    def other_pair():
        q = got2[...]
        return softmax_once(
            [
                (dot_t(q, msg[one, keys]), msg[one, values]),
                (dot_t(q, got1[one, keys]), got1[one, values]),
            ],
            True,
        )

    def own_pair():
        return softmax_once([(dot_t(qm[...], got1[one, keys]), got1[one, values])], True)

    def far_level():
        half = pl.ds(512, 64)
        qf[pl.ds(0, 128), :] = qm[head, :]
        qf[pl.ds(128, 128), :] = got2[head, :]
        qf[pl.ds(256, 64), :] = got1[half, keys]
        qf[pl.ds(320, 64), :] = got1[half, values]
        qf[pl.ds(384, 128), :] = got3[...]
        for i, col in enumerate((col1, col2, col3)):
            kf[pl.ds(128 * i, 128), :] = col[...]
        s = dot_t(qf[...], kf[:, keys])
        at = lax.broadcasted_iota(jnp.int32, (1, 384), 1)
        return softmax_once([(jnp.where(at < 128 * group, s, NEG), kf[:, values])])

    fill(local < 2, acc_2, ml_2, other_pair)
    fill((local & 1) == 1, acc_m, ml_m, own_pair)
    fill(group > 0, acc_f, ml_f, far_level)

    def give(out, terms, rows):
        m, l, acc = combine(terms)
        out[rows, :] = (acc / jnp.where(l > 0.0, l, 1.0)).astype(BF16)
        return m, l

    far2 = term(acc_f, ml_f, pl.ds(128, 128))
    m_a, l_a = give(back2, [term(acc_2, ml_2, head), far2], head)
    m_b, l_b = give(back2, [term(acc_2, ml_2, tail)], tail)
    back2[pl.ds(512, 32), :] = pack(
        jnp.concatenate([m_a, m_b], axis=0), jnp.concatenate([l_a, l_b], axis=0)
    )
    for out, first in ((back1, 256), (back3, 384)):
        m, l = give(out, [term(acc_f, ml_f, pl.ds(first, 128))], head)
        out[pl.ds(128, 16), :] = pack(m, l)
    load_acc.wait()
    load_ml.wait()
    for at in (head, tail):
        terms = [term(acc_n, ml_n, at), term(acc_m, ml_m, at)]
        if at is head:
            terms.append(term(acc_f, ml_f, head))
        m, l, acc = combine(terms)
        acc_n[at, :] = acc
        ml_n[at, :] = both(m, l)
    save_acc = pltpu.make_async_copy(acc_n, acc_o, sem.at[0])
    save_ml = pltpu.make_async_copy(ml_n, ml_o, sem.at[1])
    save_acc.start()
    save_ml.start()
    save_acc.wait()
    save_ml.wait()


def merge_kernel(near_h, acc_h, ml_h, back1, back2, back3, out, near, acc, ml, wide, sem):
    copies = [
        pltpu.make_async_copy(src, dst, sem.at[i])
        for i, (src, dst) in enumerate(((near_h, near), (acc_h, acc), (ml_h, ml)))
    ]
    for cp in copies:
        cp.start()
    for cp in copies:
        cp.wait()
    wide[...] = near[...].astype(F32)
    for c in range(4):
        at = pl.ds(128 * c, 128)
        terms = [(ml[at, :][:, 0:1], ml[at, :][:, 1:2], acc[at, :])]
        for part, rows, stat in ((back2, 128 * c, 512 + 8 * c), (back1, 0, 128), (back3, 0, 128)):
            if c and part is not back2:
                continue
            pm, plen = unpack(part[pl.ds(stat // 16 * 16, 16), :][stat % 16 : stat % 16 + 8])
            terms.append((pm, plen, part[pl.ds(rows, 128), :].astype(F32) * plen))
        top = functools.reduce(jnp.maximum, [t[0] for t in terms])
        total = 0.0
        length = 0.0
        for tm, tl, ta in terms:
            w = jnp.exp2((tm - top) * EXP_SCALE)
            length = length + tl * w
            total = total + ta * w
        wide[pl.ds(class_residue(c), 128, stride=16), :] = total / length
    out[...] = wide[...].astype(BF16)


def pieces(x):
    hi = x.astype(BF16).astype(F32)
    rest = x - hi
    mid = rest.astype(BF16).astype(F32)
    return hi, mid, (rest - mid).astype(BF16).astype(F32)


def cache_kernel(own, lens, arr, cache, out, o_s, st_s):
    z = lax.axis_index("seq")
    me = lax.axis_index("req")
    per = cache.shape[2]
    width = cache.shape[3]
    diag = lax.shift_right_logical(
        lax.broadcasted_iota(jnp.int32, (16, width), 1), 7
    ) == lax.shift_right_logical(lax.broadcasted_iota(jnp.int32, (16, width), 0), 1)
    token = lax.broadcasted_iota(jnp.int32, (16, 16), 0) & 1
    new_col = lax.broadcasted_iota(jnp.int32, (16, 16), 1)
    new_ok = (new_col <= token) & (z == 0)
    col = z * per + lax.broadcasted_iota(jnp.int32, (16, per), 1)
    row_head = lax.shift_right_logical(lax.broadcasted_iota(jnp.int32, (16, HD), 0), 1)
    lane = lax.broadcasted_iota(jnp.int32, (16, HD), 1)
    pad = jnp.zeros((14, width), F32)
    for k in range(4):
        grp, rank = rank_in_block(own, 4 * me, k)
        row = 2 * grp + rank
        q = arr[row, 0].astype(F32)
        qd = jnp.where(diag, jnp.concatenate([q] * 8, axis=0), 0.0).astype(BF16)
        kn = jnp.concatenate([arr[row, 1].astype(F32), pad], axis=0).astype(BF16)
        vn = jnp.concatenate([arr[row, 2].astype(F32), pad], axis=0).astype(BF16)
        c_ok = col < lens[4 * me + k]
        s_c = jnp.where(c_ok, dot_t(qd, cache[k, 0]), NEG)
        s_n = jnp.where(new_ok, dot_t(qd, kn), NEG)
        m = jnp.maximum(
            jnp.max(s_c, axis=1, keepdims=True), jnp.max(s_n, axis=1, keepdims=True)
        )
        p_c = jnp.where(c_ok, jnp.exp2((s_c - m) * EXP_SCALE), 0.0)
        p_n = jnp.where(new_ok, jnp.exp2((s_n - m) * EXP_SCALE), 0.0)
        l = jnp.sum(p_c, axis=1, keepdims=True) + jnp.sum(p_n, axis=1, keepdims=True)
        full = dot_n(p_c.astype(BF16), cache[k, 1]) + dot_n(p_n.astype(BF16), vn)
        o = jnp.zeros((16, HD), F32)
        for h in range(8):
            o = jnp.where(row_head == h, full[:, HD * h : HD * (h + 1)], o)
        o = o / jnp.where(l > 0.0, l, 1.0)
        st = jnp.zeros((16, HD), F32)
        for at, piece in enumerate(pieces(m) + pieces(l)):
            st = jnp.where(lane == at, piece, st)
        for h in range(8):
            o_s[pl.ds(8 * h + 2 * k, 2), :] = o[2 * h : 2 * h + 2]
            st_s[pl.ds(8 * h + 2 * k, 2), :] = st[2 * h : 2 * h + 2]
    values = o_s[...].astype(BF16)
    turned = st_s[...].T
    stats = jnp.concatenate([turned[:8, :], jnp.zeros((8, 64), F32)], axis=1).astype(BF16)
    for t in range(out.shape[0]):
        out[t, pl.ds(0, 64), :] = values
        out[t, pl.ds(64, 8), :] = stats


def project_kernel(own, got, weight, out):
    me = lax.axis_index("req")
    count = got.shape[0]
    ms, ls = [], []
    for t in range(count):
        st = got[t, pl.ds(64, 8), :].astype(F32)
        ms.append(st[0:1] + st[1:2] + st[2:3])
        ls.append(st[3:4] + st[4:5] + st[5:6])
    m = jnp.concatenate(ms, axis=0)
    l = jnp.concatenate(ls, axis=0)
    share = jnp.exp2((m - jnp.max(m, axis=0, keepdims=True)) * EXP_SCALE) * l
    share = share / jnp.sum(share, axis=0, keepdims=True)
    share = jnp.concatenate([share, jnp.zeros((128 - count, HD), F32)], axis=0).T
    total = jnp.zeros((64, HD), F32)
    for t in range(count):
        total = total + share[:64, t : t + 1] * got[t, pl.ds(0, 64), :].astype(F32)
    rows = jnp.concatenate([total[8 * h : 8 * h + 8] for h in range(8)], axis=1)
    y = dot_n(rows.astype(BF16), weight[...])
    out[...] = jnp.zeros(out.shape, BF16)
    seats = [rank_in_block(own, 4 * me, k) for k in range(4)]
    for h in range(4):
        cols = slice(64 * h, 64 * h + 64)
        lines = [
            jnp.concatenate([y[2 * k : 2 * k + 1, cols], y[2 * k + 1 : 2 * k + 2, cols]], axis=1)
            for k in range(4)
        ]
        for grp, _ in seats:
            pair = [jnp.zeros((1, HD), F32)] * 2
            for (other, rank), line in zip(seats, lines):
                for r in range(2):
                    pair[r] = jnp.where((other == grp) & (rank == r), line, pair[r])
            out[8 * h + grp] = jnp.concatenate(pair, axis=0).astype(BF16)


def settle_kernel(own, got, out):
    me = lax.axis_index("req")
    total = got[pl.ds(0, 8)].astype(F32)
    for h in range(1, 4):
        total = total + got[pl.ds(8 * h, 8)].astype(F32)
    out[...] = jnp.zeros(out.shape, BF16)
    for b in range(8):
        seats = [(own[4 * b + k], *rank_in_block(own, 4 * b, k)) for k in range(4)]
        for r in range(2):
            place = jnp.int32(-1)
            for slot, grp, rank in seats:
                place = jnp.where((grp == me) & (rank == r), slot & 15, place)
            row = total[b, r : r + 1]
            both_tokens = jnp.concatenate([row[:, :64], row[:, 64:]], axis=0).astype(BF16)

            @pl.when(place >= 0)
            def _(place=place, both_tokens=both_tokens):
                out[place] = both_tokens


def shape(dims, dtype=BF16):
    return jax.ShapeDtypeStruct(dims, dtype)


def staged(pre_qkv, cache_kv, dec_new, out_weight, owner_slot, prompt_lengths):
    qkv = jnp.swapaxes(pre_qkv, 0, 1)
    raw, sent, qm, ask, msg, far = call(
        start_kernel,
        (
            shape((3, 2048, HD)),
            shape(dec_new.shape),
            shape((512, HD)),
            shape((128, HD)),
            shape((576, 2 * HD)),
            shape((128, 2 * HD)),
        ),
        (far_memory(owner_slot), far_memory(dec_new), far_memory(qkv)),
        [hspec(), hspec(), hspec()],
        [
            SMEM((32,), jnp.int32),
            VMEM((2048, HD), F32),
            pltpu.SemaphoreType.DMA((16,)),
            pltpu.SemaphoreType.DMA((3,)),
            pltpu.SemaphoreType.DMA,
        ],
        nbytes=4000000,
    )
    arrived = lax.all_to_all(sent, "req", 0, 0, tiled=True)

    def swap(x, bits):
        return lax.ppermute(x, "seq", [(i, i ^ bits) for i in range(16)])

    def relay(x, first, stop, hop):
        return lax.ppermute(x, "seq", [(i, i + hop) for i in range(first, stop)])

    col1 = relay(far, 0, 12, 4)
    col3 = relay(far, 0, 4, 12)
    got3 = swap(ask, 3)
    got2 = swap(qm, 2)
    got1 = swap(msg, 1)
    col2 = relay(col1, 4, 12, 4)
    state = [pltpu.HBM((512, HD), F32)] * 2
    near_o, acc, ml = call(
        near_kernel,
        (pltpu.HBM((2048, HD), BF16), *state),
        (raw, qm, msg),
        [vspec()] * 3,
        [
            VMEM((2048, HD), F32),
            VMEM((2048, HD), F32),
            VMEM((2048, HD), BF16),
            VMEM((512, HD), F32),
            VMEM((512, HD), F32),
            pltpu.SemaphoreType.DMA((8,)),
            pltpu.SemaphoreType.DMA((8,)),
        ],
        flops=2 * 10**9,
        nbytes=3000000,
        trans=2 * 10**6,
        outs=[hspec()] * 3,
    )
    partial = call(
        cache_kernel,
        shape((16, 72, HD)),
        (owner_slot, prompt_lengths, arrived, cache_kv),
        [sspec(), sspec(), vspec(), vspec()],
        [VMEM((64, HD), F32), VMEM((64, HD), F32)],
        flops=10**8,
        nbytes=2000000,
    )
    parts = lax.all_to_all(partial, "seq", 0, 0, tiled=True)
    acc, ml, back1, back2, back3 = call(
        share_kernel,
        (*state, shape((144, HD)), shape((544, HD)), shape((144, HD))),
        (qm, msg, got1, got2, got3, col1, col2, col3, far_memory(acc), far_memory(ml)),
        [vspec()] * 8 + [hspec()] * 2,
        [VMEM((512, HD), F32)] * 8
        + [VMEM((512, HD), BF16), VMEM((384, 2 * HD), BF16), pltpu.SemaphoreType.DMA((2,))],
        flops=10**9,
        nbytes=4000000,
        trans=10**6,
        outs=[hspec()] * 2 + [vspec()] * 3,
    )
    back1 = swap(back1, 1)
    back3 = swap(back3, 3)
    back2 = swap(back2, 2)
    answers = call(
        project_kernel,
        shape((32, 2, HD)),
        (owner_slot, parts, out_weight),
        [sspec(), vspec(), vspec()],
        flops=10**7,
        nbytes=1000000,
    )
    results = lax.all_to_all(answers, ("head", "req"), 0, 0, tiled=True)
    prefill_out = call(
        merge_kernel,
        shape((2048, HD)),
        (far_memory(near_o), far_memory(acc), far_memory(ml), back1, back2, back3),
        [hspec()] * 3 + [vspec()] * 3,
        [
            VMEM((2048, HD), BF16),
            VMEM((512, HD), F32),
            VMEM((512, HD), F32),
            VMEM((2048, HD), F32),
            pltpu.SemaphoreType.DMA((3,)),
        ],
        flops=10**8,
        nbytes=4000000,
    )
    decode_out = call(
        settle_kernel,
        shape((16, 2, 64)),
        (owner_slot, results),
        [sspec(), vspec()],
        nbytes=100000,
    )
    return prefill_out, decode_out


def solution(mesh):
    return jax.shard_map(
        staged,
        mesh=mesh,
        in_specs=(
            P("seq", None, ("head", "req")),
            P("req", None, "seq", "head"),
            P("req", None, None, "head"),
            P("head", "seq"),
            P(),
            P(),
        ),
        out_specs=(P("seq", ("head", "req")), P("req", None, ("seq", "head"))),
        check_vma=False,
    )
```
